32 devices in a mesh: seq: 16 (over z, y, x), head: 2 (over core).
Axes of the slice: x: 2, y: 2, z: 4, core: 2. Of those that a mesh axis runs over, the one named last changes fastest.
Arguments:
- queries: bfloat16 [4096, 4096], P('seq', 'head'), may hold values from -1.796875 to 1.796875
- key_rows: bfloat16 [4096, 4096], P('seq', 'head'), may hold values from -1.796875 to 1.796875
- values: bfloat16 [4096, 4096], P('seq', 'head'), may hold values from -100 to 100
- out_weight: bfloat16 [4096, 4096], P('head', 'seq'), may hold values from -0.125 to 0.125
- out_grad: bfloat16 [4096, 4096], P('seq', 'head'), may hold values from -6 to 6
Outputs:
- mixed: bfloat16 [4096, 4096], P('seq', 'head')
- query_grad: bfloat16 [4096, 4096], P('seq', 'head')
- key_grad: bfloat16 [4096, 4096], P('seq', 'head')
- value_grad: bfloat16 [4096, 4096], P('seq', 'head')
The draws below stay inside these ranges and needn't reach their ends.
All inputs are finite; a program needn't handle non-finite values.
Results may differ from the reference program's by a relative error of at most 0.014.
Values may be sent and summed in bfloat16 or wider, within the bound.
A program may use at most 128 MiB of HBM per device.

```python
import math
import jax
import jax.numpy as jnp
from jax import lax

D = 4096
HEADS = 32
HEAD_DIM = 128
TOK_DEV = 256
TOKENS = 4096
INNER = 4096
N_HEAD = 2


def draw_values(key, part):
    row_key = jax.random.fold_in(key, 11)
    col_key = jax.random.fold_in(key, 12)
    entry_key = jax.random.fold_in(key, 13)
    row_scale = jnp.exp(jax.random.uniform(row_key, (TOKENS, 1), jnp.float32) * math.log(10.0))
    col_scale = jnp.exp(jax.random.uniform(col_key, (1, INNER), jnp.float32) * math.log(10.0))
    entries = jnp.clip(jax.random.normal(entry_key, (TOKENS, INNER), jnp.float32), -4.0, 4.0)
    return (entries * row_scale * col_scale / 4.0).astype(jnp.bfloat16)


def with_spikes(drawn, stream_key, source, target, shards_of, factor):
    owner, partner = [(jnp.arange(drawn.shape[axis_at]) // (drawn.shape[axis_at] // shards_of)).reshape([-1 if axis == axis_at else 1 for axis in range(drawn.ndim)]) for axis_at in (source, target)]
    chosen = jax.random.permutation(stream_key, shards_of)[partner]
    strong = (owner == chosen) | (owner == (partner + shards_of // 2) % shards_of)
    return jnp.where(strong, factor * drawn, drawn)


def block_scale(key, dims, split, low, high):
    def one(position, blocks):
        steps = jax.random.uniform(jax.random.fold_in(jax.random.fold_in(key, 6), position), (blocks,), jnp.float32, low / len(split), high / len(split))
        return jnp.repeat(jnp.exp(steps), dims[position] // blocks).reshape((-1,) + (1,) * (len(dims) - position - 1))

    loudness = one(*split[0])
    for cut in split[1:]:
        loudness = loudness * one(*cut)
    return loudness


def gaussian(key, extent, width, reach, shards=(), kind=jnp.bfloat16):
    gain = block_scale(key, extent, shards, -0.22, 0.18) if shards else 1.0
    array = jax.random.normal(key, extent, jnp.float32) * width * gain
    return jnp.minimum(jnp.maximum(array, -reach), reach).astype(kind)


def heavy_noise(rng, dims, width, reach, pieces, heavy, dtype=jnp.bfloat16):
    array = width * jax.random.normal(rng, dims, jnp.float32)
    if pieces:
        array = array * block_scale(rng, dims, pieces, -0.22, 0.18)
    return jnp.clip(with_spikes(array, jax.random.fold_in(rng, 3), *heavy), -reach, reach).astype(dtype)


def setup_inputs(seed: int = 0) -> dict:
    streams_of = jax.random.split(jax.random.key(seed), 6)
    return {
        "queries": gaussian(streams_of[0], (TOKENS, INNER), 0.3, 1.796875, ((0, 16), (1, 2))),
        "key_rows": gaussian(streams_of[1], (TOKENS, INNER), 0.3, 1.796875, ((0, 16), (1, 2))),
        "values": draw_values(jax.random.fold_in(streams_of[5], 71), 0),
        "out_weight": heavy_noise(streams_of[3], (INNER, D), INNER ** -0.5, 0.125, ((0, 2), (1, 16)), (0, 1, 16, 2.0)),
        "out_grad": gaussian(streams_of[4], (TOKENS, D), 1.0, 6.0, ((0, 16), (1, 2))),
    }


def rounded(tensor):
    return lax.optimization_barrier(tensor.astype(jnp.bfloat16)).astype(jnp.float32)

def lower_mask(length):
    row_ids = lax.broadcasted_iota(jnp.int32, (length, length), 0)
    col_ids = lax.broadcasted_iota(jnp.int32, (length, length), 1)
    return row_ids >= col_ids

def reference(queries, key_rows, values, out_weight, out_grad):
    block_count = TOKENS // TOK_DEV
    head_shape = (block_count, TOK_DEV, HEADS, HEAD_DIM)
    query_blocks = queries.reshape(head_shape)
    key_blocks = key_rows.reshape(head_shape)
    value_blocks = values.reshape(head_shape)
    grad_blocks = out_grad.reshape(block_count, TOK_DEV, D)
    causal = lower_mask(TOK_DEV)[None]
    group_width = INNER // N_HEAD

    def state_of(packed):
        key_part, value_part = packed
        return jnp.einsum('shd,she->hde', key_part.astype(jnp.float32), value_part.astype(jnp.float32))
    local_state = lax.map(state_of, (key_blocks, value_blocks))
    running_state = jnp.cumsum(local_state, axis=0)
    prefix_state = jnp.concatenate([jnp.zeros_like(local_state[:1]), running_state[:-1]], axis=0)

    def forward(packed):
        query_part, key_part, value_part, prefix_part, grad_part = packed
        query_wide = query_part.astype(jnp.float32)
        key_wide = key_part.astype(jnp.float32)
        value_wide = value_part.astype(jnp.float32)
        scores = jnp.einsum('thd,shd->hts', query_wide, key_wide)
        weights = rounded(jnp.where(causal, scores, 0.0))
        numerator = jnp.einsum('hts,she->the', weights, value_wide) + jnp.einsum('thd,hde->the', query_wide, rounded(prefix_part))
        spread = jnp.sqrt(lax.optimization_barrier(jnp.mean(numerator * numerator, axis=-1, keepdims=True)) + 1e-06)
        normed = numerator / spread
        attended = normed.astype(jnp.bfloat16).reshape(TOK_DEV, INNER)
        summed = jnp.zeros((TOK_DEV, D), jnp.float32)
        for group in range(N_HEAD):
            first_col = group * group_width
            term = jnp.dot(attended[:, first_col:first_col + group_width], out_weight[first_col:first_col + group_width], preferred_element_type=jnp.float32)
            summed = summed + rounded(term)
        layer_out = summed.astype(jnp.bfloat16)
        out_dir = lax.dot_general(grad_part, out_weight, (((1,), (1,)), ((), ())), preferred_element_type=jnp.float32)
        out_dir = out_dir.reshape(TOK_DEV, HEADS, HEAD_DIM)
        along_dir = lax.optimization_barrier(jnp.mean(out_dir * normed, axis=-1, keepdims=True))
        numer_grad = rounded((out_dir - normed * along_dir) / spread)
        local_grad = jnp.einsum('thd,the->hde', query_wide, numer_grad)
        return (layer_out, numer_grad, local_grad)
    layer_out, numer_grad, local_grad = lax.map(forward, (query_blocks, key_blocks, value_blocks, prefix_state, grad_blocks))
    reversed_sum = jnp.cumsum(local_grad[::-1], axis=0)[::-1]
    suffix_grad = jnp.concatenate([reversed_sum[1:], jnp.zeros_like(local_grad[:1])], axis=0)

    def backward(packed):
        query_part, key_part, value_part, prefix_part, suffix_part, numer_part = packed
        query_wide = query_part.astype(jnp.float32)
        key_wide = key_part.astype(jnp.float32)
        value_wide = value_part.astype(jnp.float32)
        scores = jnp.einsum('thd,shd->hts', query_wide, key_wide)
        weights = rounded(jnp.where(causal, scores, 0.0))
        pair_scores = jnp.einsum('the,she->hts', numer_part, value_wide)
        pair_low = rounded(jnp.where(causal, pair_scores, 0.0))
        prefix_low = rounded(prefix_part)
        suffix_low = rounded(suffix_part)
        query_out = jnp.einsum('hts,shd->thd', pair_low, key_wide) + jnp.einsum('the,hde->thd', numer_part, prefix_low)
        key_out = jnp.einsum('hts,thd->shd', pair_low, query_wide) + jnp.einsum('she,hde->shd', value_wide, suffix_low)
        value_out = jnp.einsum('hts,the->she', weights, numer_part) + jnp.einsum('shd,hde->she', key_wide, suffix_low)
        flat_shape = (TOK_DEV, INNER)
        return (query_out.reshape(flat_shape).astype(jnp.bfloat16), key_out.reshape(flat_shape).astype(jnp.bfloat16), value_out.reshape(flat_shape).astype(jnp.bfloat16))
    query_grad, key_grad, value_grad = lax.map(backward, (query_blocks, key_blocks, value_blocks, prefix_state, suffix_grad, numer_grad))
    return (layer_out.reshape(TOKENS, D), query_grad.reshape(TOKENS, INNER), key_grad.reshape(TOKENS, INNER), value_grad.reshape(TOKENS, INNER))
```

```python
import functools

import jax
import jax.numpy as jnp
from jax import lax
from jax.experimental import pallas as pl
from jax.experimental.pallas import tpu as pltpu
from jax.sharding import PartitionSpec as P

HEAD_DIM = 128
MESH = pl.DeviceIdType.MESH
PLANE = 4


def prefix_2(value, axis, combine, identity):
    length, position = (lax.axis_size(axis), lax.axis_index(axis))
    everything = lax.all_gather(value, axis)
    start = jnp.broadcast_to(jnp.asarray(identity, value.dtype), value.shape)

    def hop(k, before):
        reached = k < position
        new = combine(before, everything[k])
        return jnp.where(reached, new, before)

    return lax.fori_loop(0, length, hop, start)


def prefix_3(value, axis, combine, identity):
    length, position = (lax.axis_size(axis), lax.axis_index(axis))
    everything = lax.all_gather(value.astype(jnp.bfloat16), axis)
    start = jnp.broadcast_to(jnp.asarray(identity, value.dtype), value.shape)

    def hop(k, before):
        at = length - 1 - k
        reached = at > position
        new = combine(before, everything[at].astype(value.dtype))
        return jnp.where(reached, new, before)

    return lax.fori_loop(0, length, hop, start)


def lower_mask(length):
    row_ids = lax.broadcasted_iota(jnp.int32, (length, length), 0)
    col_ids = lax.broadcasted_iota(jnp.int32, (length, length), 1)
    return row_ids >= col_ids


def add_states(earlier, latter):
    return earlier + latter


def contract_cols(left_side, right_side):
    return lax.dot_general(
        left_side, right_side, (((1,), (1,)), ((), ())), preferred_element_type=jnp.float32
    )


def contract_rows(left_side, right_side):
    return lax.dot_general(
        left_side, right_side, (((0,), (0,)), ((), ())), preferred_element_type=jnp.float32
    )


def contract_mid(left_side, right_side):
    return jnp.dot(left_side, right_side, preferred_element_type=jnp.float32)


def per_device(queries, key_rows, values, out_weight, out_grad):
    length = queries.shape[0]
    heads_here = queries.shape[1] // HEAD_DIM
    query_heads = queries.reshape(length, heads_here, HEAD_DIM)
    key_heads = key_rows.reshape(length, heads_here, HEAD_DIM)
    value_heads = values.reshape(length, heads_here, HEAD_DIM)
    causal = lower_mask(length)[None]
    local_state = jnp.einsum(
        "shd,she->hde", key_heads, value_heads, preferred_element_type=jnp.float32
    )
    prefix = prefix_2(local_state, "seq", add_states, jnp.zeros_like(local_state))
    prefix_low = prefix.astype(jnp.bfloat16)
    scores = jnp.einsum("thd,shd->hts", query_heads, key_heads, preferred_element_type=jnp.float32)
    weights = jnp.where(causal, scores, 0.0).astype(jnp.bfloat16)
    numerator = jnp.einsum("hts,she->the", weights, value_heads, preferred_element_type=jnp.float32)
    numerator = numerator + jnp.einsum(
        "thd,hde->the", query_heads, prefix_low, preferred_element_type=jnp.float32
    )
    spread = jnp.sqrt(jnp.mean(numerator * numerator, axis=-1, keepdims=True) + 1e-06)
    normed = numerator / spread
    attended = normed.astype(jnp.bfloat16).reshape(length, heads_here * HEAD_DIM)
    full_weight = lax.all_gather(out_weight, "seq", axis=1, tiled=True)
    partial_value = jnp.dot(attended, full_weight, preferred_element_type=jnp.float32)
    layer_out = lax.psum_scatter(
        partial_value.astype(jnp.bfloat16), "head", scatter_dimension=1, tiled=True
    )
    out_dir = contract_cols(lax.all_gather(out_grad, "head", axis=1, tiled=True), full_weight)
    out_dir = out_dir.reshape(length, heads_here, HEAD_DIM)
    along_dir = jnp.mean(out_dir * normed, axis=-1, keepdims=True)
    numer_grad = ((out_dir - normed * along_dir) / spread).astype(jnp.bfloat16)
    local_grad = jnp.einsum(
        "thd,the->hde", query_heads, numer_grad, preferred_element_type=jnp.float32
    )
    suffix = prefix_3(local_grad, "seq", add_states, jnp.zeros_like(local_grad))
    suffix_low = suffix.astype(jnp.bfloat16)
    pair_scores = jnp.einsum(
        "the,she->hts", numer_grad, value_heads, preferred_element_type=jnp.float32
    )
    pair_low = jnp.where(causal, pair_scores, 0.0).astype(jnp.bfloat16)
    query_out = jnp.einsum("hts,shd->thd", pair_low, key_heads, preferred_element_type=jnp.float32)
    query_out = query_out + jnp.einsum(
        "the,hde->thd", numer_grad, prefix_low, preferred_element_type=jnp.float32
    )
    key_out = jnp.einsum("hts,thd->shd", pair_low, query_heads, preferred_element_type=jnp.float32)
    key_out = key_out + jnp.einsum(
        "she,hde->shd", value_heads, suffix_low, preferred_element_type=jnp.float32
    )
    value_out = jnp.einsum("hts,the->she", weights, numer_grad, preferred_element_type=jnp.float32)
    value_out = value_out + jnp.einsum(
        "shd,hde->she", key_heads, suffix_low, preferred_element_type=jnp.float32
    )
    flat_shape = (length, heads_here * HEAD_DIM)
    return (
        layer_out,
        query_out.reshape(flat_shape).astype(jnp.bfloat16),
        key_out.reshape(flat_shape).astype(jnp.bfloat16),
        value_out.reshape(flat_shape).astype(jnp.bfloat16),
    )


def visit_tables(planes):
    rows = []
    for own in range(planes):
        near_low = own < planes - 1 - own
        rows.append(sorted(range(planes), key=lambda other: (abs(other - own), (other > own) == near_low)))
    return rows


def pick(table, position):
    found = jnp.int32(table[0])
    for at in range(1, len(table)):
        found = jnp.where(position == at, jnp.int32(table[at]), found)
    return found


def kernel(
    blocks, q_ref, k_ref, v_ref, w_ref, g_ref,
    mixed_ref, dq_ref, dk_ref, dv_ref,
    w_all, g_all, st_send, st_recv, pre_send, prefix, lg_send, lg_recv, suf_send, suffix,
    out_dir, normed, inv_spread, weights, attended, p_own, p_send, p_recv, ng, k_part, v_part,
    w_recv_sem, wx_sem, wy_sem, wz_sem, local_sem, g_sem, a_send_sem, a_recv_sem, p_send_sem, p_recv_sem,
):
    me = lax.axis_index("seq")
    core = lax.axis_index("head")
    other = 1 - core
    planes = blocks // PLANE
    spot = lax.rem(me, PLANE)
    level = me // PLANE
    bit_x, bit_y = lax.rem(spot, 2), spot // 2
    spot_x = spot + 1 - 2 * bit_x
    spot_y = spot + 2 - 4 * bit_y
    spot_d = spot_x + 2 - 4 * bit_y
    length, width = q_ref.shape
    heads = width // HEAD_DIM
    rows, cols = w_ref.shape
    half = rows // 2
    per_core = blocks // 2

    def at_seq(position):
        return (position, core)

    nbr_x = level * PLANE + spot_x
    nbr_y = level * PLANE + spot_y

    barrier = pltpu.get_barrier_semaphore()

    def greet(i, carry):
        pl.semaphore_signal(barrier, inc=1, device_id=at_seq(lax.rem(me + i, blocks)), device_id_type=MESH)
        return carry

    lax.fori_loop(1, blocks, greet, 0)
    pl.semaphore_signal(barrier, inc=1, device_id=(me, other), device_id_type=MESH)

    own_w = pltpu.make_async_copy(w_ref, w_all.at[me], local_sem.at[0])
    own_g = pltpu.make_async_copy(g_ref, g_all.at[core], local_sem.at[1])
    own_w.start()
    own_g.start()

    def head_cols(h):
        return pl.ds(pl.multiple_of(h * HEAD_DIM, HEAD_DIM), HEAD_DIM)

    def make_state(h, carry):
        c = head_cols(h)
        st_send[h] = contract_rows(k_ref[:, c], v_ref[:, c]).astype(jnp.bfloat16)
        return carry

    lax.fori_loop(0, heads, make_state, 0)
    st_recv[me] = st_send[me]

    pl.semaphore_wait(barrier, blocks)

    def exchange(src, dst, kind, start):
        def one(i, carry):
            peer = lax.rem(me + i, blocks)
            copy = pltpu.make_async_remote_copy(
                src_ref=src.at[peer], dst_ref=dst.at[me],
                send_sem=a_send_sem.at[kind, peer], recv_sem=a_recv_sem.at[kind, me],
                device_id=at_seq(peer), device_id_type=MESH,
            )
            if start:
                copy.start()
            else:
                copy.wait_send()
            return carry

        lax.fori_loop(1, blocks, one, 0)

    def arrived(src, dst, kind):
        def one(i, carry):
            peer = lax.rem(me + i, blocks)
            pltpu.make_async_remote_copy(
                src_ref=src.at[me], dst_ref=dst.at[peer],
                send_sem=a_send_sem.at[kind, me], recv_sem=a_recv_sem.at[kind, peer],
                device_id=at_seq(peer), device_id_type=MESH,
            ).wait_recv()
            return carry

        lax.fori_loop(1, blocks, one, 0)

    g_copy = pltpu.make_async_remote_copy(
        src_ref=g_ref, dst_ref=g_all.at[core], send_sem=g_sem.at[0], recv_sem=g_sem.at[1],
        device_id=(me, other), device_id_type=MESH,
    )
    g_copy.start()
    exchange(st_send, st_recv, 0, True)

    def piece(block, part, sems, target, own=False):
        span = pl.ds(part * half, half)
        return pltpu.make_async_remote_copy(
            src_ref=w_ref.at[span] if own else w_all.at[block, span],
            dst_ref=w_all.at[block, span],
            send_sem=sems.at[block, part], recv_sem=w_recv_sem.at[block, part],
            device_id=at_seq(target), device_id_type=MESH,
        )

    up_ok = level + 1 < planes
    down_ok = level > 0
    up = jnp.minimum(me + PLANE, blocks - PLANE + spot)
    down = jnp.maximum(me - PLANE, spot)

    for part in range(2):
        piece(me, part, wx_sem, nbr_x, True).start()
        piece(me, part, wy_sem, nbr_y, True).start()

        @pl.when(up_ok)
        def _():
            piece(me, part, wz_sem.at[0], up, True).start()

        @pl.when(down_ok)
        def _():
            piece(me, part, wz_sem.at[1], down, True).start()

    tables = visit_tables(planes)
    order = [pick([tables[z][k] for z in range(planes)], level) for k in range(planes)]

    def column_step(k, finish=False):
        plane = order[k]
        block = plane * PLANE + spot
        going_up = plane < level
        for part in range(2):
            if not finish:
                piece(block, part, wx_sem, nbr_x).wait_recv()
                piece(block, part, wx_sem, nbr_x).start()
                piece(block, part, wy_sem, nbr_y).start()

            @pl.when(jnp.logical_and(going_up, up_ok))
            def _():
                copy = piece(block, part, wz_sem.at[0], up)
                copy.wait_send() if finish else copy.start()

            @pl.when(jnp.logical_and(jnp.logical_not(going_up), down_ok))
            def _():
                copy = piece(block, part, wz_sem.at[1], down)
                copy.wait_send() if finish else copy.start()

            if finish:
                piece(block, part, wx_sem, nbr_x).wait_send()
                piece(block, part, wy_sem, nbr_y).wait_send()

    def relay_step(k, finish=False):
        plane = order[k]
        to_x = piece(plane * PLANE + spot_y, 0, wx_sem, nbr_x)
        to_y = piece(plane * PLANE + spot_x, 1, wy_sem, nbr_y)
        for copy in (to_x, to_y):
            if finish:
                copy.wait_send()
            else:
                copy.wait_recv()
                copy.start()

    def settle(k):
        plane = order[k]
        for where, part in ((spot_y, 1), (spot_x, 0), (spot_d, 0), (spot_d, 1)):
            piece(plane * PLANE + where, part, wx_sem, nbr_x).wait_recv()

    causal = lower_mask(length)

    def score_step(h, carry):
        c = head_cols(h)
        kept = jnp.where(causal, contract_cols(q_ref[:, c], k_ref[:, c]), 0.0).astype(jnp.bfloat16)
        weights[h] = kept
        normed[h] = contract_mid(kept, v_ref[:, c])
        return carry

    def norm_step(h, carry):
        c = head_cols(h)
        numerator = normed[h] + contract_mid(q_ref[:, c], prefix[h])
        inv = 1.0 / jnp.sqrt(jnp.mean(numerator * numerator, axis=-1, keepdims=True) + 1e-06)
        value = numerator * inv
        normed[h] = value
        inv_spread[h] = jnp.broadcast_to(inv, (length, HEAD_DIM))
        attended[:, c] = value.astype(jnp.bfloat16)
        return carry

    tile = cols
    n_tiles = rows // tile

    def grad_cols(block):
        return g_all[block // per_core, :, pl.ds(pl.multiple_of(lax.rem(block, per_core) * cols, cols), cols)]

    def direction_step(k):
        base = order[k] * PLANE

        def one(n, carry):
            span = pl.ds(pl.multiple_of(n * tile, tile), tile)
            total = contract_cols(grad_cols(base), w_all[base, span])
            for s in range(1, PLANE):
                total = total + contract_cols(grad_cols(base + s), w_all[base + s, span])
            if k > 0:
                total = total + out_dir[:, span]
            out_dir[:, span] = total
            return carry

        lax.fori_loop(0, n_tiles, one, 0)

    def p_copy(slot):
        return pltpu.make_async_remote_copy(
            src_ref=p_send.at[slot], dst_ref=p_recv.at[slot],
            send_sem=p_send_sem.at[slot], recv_sem=p_recv_sem.at[slot],
            device_id=(me, other), device_id_type=MESH,
        )

    def partial_step(k):
        def one(s, carry):
            block = order[k] * PLANE + s
            term = contract_mid(attended[...], w_all[block]).astype(jnp.bfloat16)
            slot = lax.rem(block, per_core)

            @pl.when(block // per_core == core)
            def _():
                p_own[slot] = term

            @pl.when(block // per_core != core)
            def _():
                p_send[slot] = term
                p_copy(slot).start()

            return carry

        lax.fori_loop(0, PLANE, one, 0)

    lax.fori_loop(0, heads, score_step, 0)
    arrived(st_send, st_recv, 0)

    def before_step(b, total):
        low = total.astype(jnp.bfloat16)
        pre_send[b] = low

        @pl.when(b == me)
        def _():
            prefix[me] = low

        return total + st_recv[b].astype(jnp.float32)

    lax.fori_loop(0, blocks, before_step, jnp.zeros((HEAD_DIM, HEAD_DIM), jnp.float32))
    exchange(pre_send, prefix, 1, True)

    for k in range(1, planes + 1):
        if k < planes:
            column_step(k)
        relay_step(k - 1)
        if k == 1:
            own_w.wait()
            own_g.wait()
            g_copy.wait()
        if k == 2:
            arrived(pre_send, prefix, 1)
            lax.fori_loop(0, heads, norm_step, 0)
        if k >= 2:
            settle(k - 2)
            direction_step(k - 2)
            partial_step(k - 2)
    settle(planes - 1)
    direction_step(planes - 1)

    def numer_step(h, carry):
        c = head_cols(h)
        toward, unit = out_dir[:, c], normed[h]
        along = jnp.mean(toward * unit, axis=-1, keepdims=True)
        low = ((toward - unit * along) * inv_spread[h]).astype(jnp.bfloat16)
        ng[:, c] = low
        lg_send[h] = contract_rows(q_ref[:, c], low).astype(jnp.bfloat16)
        return carry

    lax.fori_loop(0, heads, numer_step, 0)
    lg_recv[me] = lg_send[me]
    exchange(lg_send, lg_recv, 2, True)
    partial_step(planes - 1)
    arrived(lg_send, lg_recv, 2)

    def after_step(i, total):
        b = blocks - 1 - i
        low = total.astype(jnp.bfloat16)
        suf_send[b] = low

        @pl.when(b == me)
        def _():
            suffix[me] = low

        return total + lg_recv[b].astype(jnp.float32)

    lax.fori_loop(0, blocks, after_step, jnp.zeros((HEAD_DIM, HEAD_DIM), jnp.float32))
    exchange(suf_send, suffix, 3, True)

    def pair_step(h, carry):
        c = head_cols(h)
        low = ng[:, c]
        pair = jnp.where(causal, contract_cols(low, v_ref[:, c]), 0.0).astype(jnp.bfloat16)
        dq_ref[:, c] = (contract_mid(pair, k_ref[:, c]) + contract_cols(low, prefix[h])).astype(jnp.bfloat16)
        k_part[h] = contract_rows(pair, q_ref[:, c])
        v_part[h] = contract_rows(weights[h], low)
        return carry

    lax.fori_loop(0, heads, pair_step, 0)

    def mix_step(slot, carry):
        p_copy(slot).wait()
        c = pl.ds(pl.multiple_of(slot * cols, cols), cols)
        mixed_ref[:, c] = (p_own[slot].astype(jnp.float32) + p_recv[slot].astype(jnp.float32)).astype(jnp.bfloat16)
        return carry

    lax.fori_loop(0, per_core, mix_step, 0)
    arrived(suf_send, suffix, 3)

    def last_step(h, carry):
        c = head_cols(h)
        dk_ref[:, c] = (k_part[h] + contract_cols(v_ref[:, c], suffix[h])).astype(jnp.bfloat16)
        dv_ref[:, c] = (v_part[h] + contract_mid(k_ref[:, c], suffix[h])).astype(jnp.bfloat16)
        return carry

    lax.fori_loop(0, heads, last_step, 0)

    for part in range(2):
        piece(me, part, wx_sem, nbr_x, True).wait_send()
        piece(me, part, wy_sem, nbr_y, True).wait_send()

        @pl.when(up_ok)
        def _():
            piece(me, part, wz_sem.at[0], up, True).wait_send()

        @pl.when(down_ok)
        def _():
            piece(me, part, wz_sem.at[1], down, True).wait_send()

    for k in range(planes):
        if k:
            column_step(k, True)
        relay_step(k, True)
    exchange(st_send, st_recv, 0, False)
    exchange(pre_send, prefix, 1, False)
    exchange(lg_send, lg_recv, 2, False)
    exchange(suf_send, suffix, 3, False)


def fused(blocks, queries, key_rows, values, out_weight, out_grad):
    length, width = queries.shape
    heads = width // HEAD_DIM
    rows, cols = out_weight.shape
    per_core = blocks // 2
    low, wide = jnp.bfloat16, jnp.float32
    state = pltpu.VMEM((blocks, HEAD_DIM, HEAD_DIM), low)
    by_head = pltpu.VMEM((heads, length, HEAD_DIM), wide)
    flat = pltpu.VMEM((length, width), low)
    parts = pltpu.VMEM((per_core, length, cols), low)
    dma = pltpu.SemaphoreType.DMA
    out = jax.ShapeDtypeStruct((length, width), low)
    vmem, anywhere = pl.BlockSpec(memory_space=pltpu.VMEM), pl.BlockSpec(memory_space=pl.ANY)
    return pl.pallas_call(
        functools.partial(kernel, blocks),
        out_shape=(out, out, out, out),
        in_specs=[vmem, vmem, vmem, anywhere, anywhere],
        out_specs=(vmem, vmem, vmem, vmem),
        scratch_shapes=[
            pltpu.VMEM((blocks, rows, cols), low),
            pltpu.VMEM((2, length, width), low),
            state, state, state, state, state, state, state, state,
            pltpu.VMEM((length, rows), wide),
            by_head, by_head,
            pltpu.VMEM((heads, length, length), low),
            flat, parts, parts, parts, flat, by_head, by_head,
            dma((blocks, 2)), dma((blocks, 2)), dma((blocks, 2)), dma((2, blocks, 2)),
            dma((2,)), dma((2,)), dma((4, blocks)), dma((4, blocks)), dma((per_core,)), dma((per_core,)),
        ],
        compiler_params=pltpu.CompilerParams(
            collective_id=0, has_side_effects=True, vmem_limit_bytes=60 * 2**20
        ),
    )(queries, key_rows, values, out_weight, out_grad)


def solution(mesh):
    blocks, cores = mesh.shape["seq"], mesh.shape["head"]

    def step(queries, key_rows, values, out_weight, out_grad):
        heads = queries.shape[1] // HEAD_DIM
        fits = cores == 2 and blocks % PLANE == 0 and heads == blocks and out_weight.shape[1] % 128 == 0
        fits = fits and out_weight.shape[0] == queries.shape[1] and out_weight.shape[0] % out_weight.shape[1] == 0
        if fits and out_weight.shape[1] * blocks == queries.shape[1] * cores:
            return fused(blocks, queries, key_rows, values, out_weight, out_grad)
        return per_device(queries, key_rows, values, out_weight, out_grad)

    placed = (
        P("seq", "head"),
        P("seq", "head"),
        P("seq", "head"),
        P("head", "seq"),
        P("seq", "head"),
    )
    return jax.shard_map(
        step,
        mesh=mesh,
        in_specs=placed,
        out_specs=(P("seq", "head"), P("seq", "head"), P("seq", "head"), P("seq", "head")),
        check_vma=False,
    )
```

```python
import functools

import jax
import jax.numpy as jnp
from jax import lax
from jax.experimental import pallas as pl
from jax.experimental.pallas import tpu as pltpu
from jax.sharding import PartitionSpec as P

HEAD_DIM = 128
MESH = pl.DeviceIdType.MESH
PLANE = 4


def prefix_2(value, axis, combine, identity):
    length, position = (lax.axis_size(axis), lax.axis_index(axis))
    everything = lax.all_gather(value, axis)
    start = jnp.broadcast_to(jnp.asarray(identity, value.dtype), value.shape)

    def hop(k, before):
        reached = k < position
        new = combine(before, everything[k])
        return jnp.where(reached, new, before)

    return lax.fori_loop(0, length, hop, start)


def prefix_3(value, axis, combine, identity):
    length, position = (lax.axis_size(axis), lax.axis_index(axis))
    everything = lax.all_gather(value.astype(jnp.bfloat16), axis)
    start = jnp.broadcast_to(jnp.asarray(identity, value.dtype), value.shape)

    def hop(k, before):
        at = length - 1 - k
        reached = at > position
        new = combine(before, everything[at].astype(value.dtype))
        return jnp.where(reached, new, before)

    return lax.fori_loop(0, length, hop, start)


def lower_mask(length):
    row_ids = lax.broadcasted_iota(jnp.int32, (length, length), 0)
    col_ids = lax.broadcasted_iota(jnp.int32, (length, length), 1)
    return row_ids >= col_ids


def add_states(earlier, latter):
    return earlier + latter


def contract_cols(left_side, right_side):
    return lax.dot_general(
        left_side, right_side, (((1,), (1,)), ((), ())), preferred_element_type=jnp.float32
    )


def contract_rows(left_side, right_side):
    return lax.dot_general(
        left_side, right_side, (((0,), (0,)), ((), ())), preferred_element_type=jnp.float32
    )


def contract_mid(left_side, right_side):
    return jnp.dot(left_side, right_side, preferred_element_type=jnp.float32)


def per_device(queries, key_rows, values, out_weight, out_grad):
    length = queries.shape[0]
    heads_here = queries.shape[1] // HEAD_DIM
    query_heads = queries.reshape(length, heads_here, HEAD_DIM)
    key_heads = key_rows.reshape(length, heads_here, HEAD_DIM)
    value_heads = values.reshape(length, heads_here, HEAD_DIM)
    causal = lower_mask(length)[None]
    local_state = jnp.einsum(
        "shd,she->hde", key_heads, value_heads, preferred_element_type=jnp.float32
    )
    prefix = prefix_2(local_state, "seq", add_states, jnp.zeros_like(local_state))
    prefix_low = prefix.astype(jnp.bfloat16)
    scores = jnp.einsum("thd,shd->hts", query_heads, key_heads, preferred_element_type=jnp.float32)
    weights = jnp.where(causal, scores, 0.0).astype(jnp.bfloat16)
    numerator = jnp.einsum("hts,she->the", weights, value_heads, preferred_element_type=jnp.float32)
    numerator = numerator + jnp.einsum(
        "thd,hde->the", query_heads, prefix_low, preferred_element_type=jnp.float32
    )
    spread = jnp.sqrt(jnp.mean(numerator * numerator, axis=-1, keepdims=True) + 1e-06)
    normed = numerator / spread
    attended = normed.astype(jnp.bfloat16).reshape(length, heads_here * HEAD_DIM)
    full_weight = lax.all_gather(out_weight, "seq", axis=1, tiled=True)
    partial_value = jnp.dot(attended, full_weight, preferred_element_type=jnp.float32)
    layer_out = lax.psum_scatter(
        partial_value.astype(jnp.bfloat16), "head", scatter_dimension=1, tiled=True
    )
    out_dir = contract_cols(lax.all_gather(out_grad, "head", axis=1, tiled=True), full_weight)
    out_dir = out_dir.reshape(length, heads_here, HEAD_DIM)
    along_dir = jnp.mean(out_dir * normed, axis=-1, keepdims=True)
    numer_grad = ((out_dir - normed * along_dir) / spread).astype(jnp.bfloat16)
    local_grad = jnp.einsum(
        "thd,the->hde", query_heads, numer_grad, preferred_element_type=jnp.float32
    )
    suffix = prefix_3(local_grad, "seq", add_states, jnp.zeros_like(local_grad))
    suffix_low = suffix.astype(jnp.bfloat16)
    pair_scores = jnp.einsum(
        "the,she->hts", numer_grad, value_heads, preferred_element_type=jnp.float32
    )
    pair_low = jnp.where(causal, pair_scores, 0.0).astype(jnp.bfloat16)
    query_out = jnp.einsum("hts,shd->thd", pair_low, key_heads, preferred_element_type=jnp.float32)
    query_out = query_out + jnp.einsum(
        "the,hde->thd", numer_grad, prefix_low, preferred_element_type=jnp.float32
    )
    key_out = jnp.einsum("hts,thd->shd", pair_low, query_heads, preferred_element_type=jnp.float32)
    key_out = key_out + jnp.einsum(
        "she,hde->shd", value_heads, suffix_low, preferred_element_type=jnp.float32
    )
    value_out = jnp.einsum("hts,the->she", weights, numer_grad, preferred_element_type=jnp.float32)
    value_out = value_out + jnp.einsum(
        "shd,hde->she", key_heads, suffix_low, preferred_element_type=jnp.float32
    )
    flat_shape = (length, heads_here * HEAD_DIM)
    return (
        layer_out,
        query_out.reshape(flat_shape).astype(jnp.bfloat16),
        key_out.reshape(flat_shape).astype(jnp.bfloat16),
        value_out.reshape(flat_shape).astype(jnp.bfloat16),
    )


def visit_tables(planes):
    half, rows = planes // 2, []
    for own in range(planes):
        rows.append(sorted(range(planes), key=lambda other: (other // half != own // half, abs(other - own))))
    return rows


def pick(table, position):
    found = jnp.int32(table[0])
    for at in range(1, len(table)):
        found = jnp.where(position == at, jnp.int32(table[at]), found)
    return found


def kernel(
    blocks, q_ref, k_ref, v_ref, w_ref, g_ref,
    mixed_ref, dq_ref, dk_ref, dv_ref,
    w_all, g_all, st_send, st_recv, pre_send, prefix, lg_send, lg_recv, suf_send, suffix,
    out_dir, normed, inv_spread, weights, attended, p_own, p_send, p_recv, ng, k_part, v_part,
    w_recv_sem, wx_sem, wy_sem, wz_sem, local_sem, g_sem, a_send_sem, a_recv_sem, p_send_sem, p_recv_sem,
):
    me = lax.axis_index("seq")
    core = lax.axis_index("head")
    other = 1 - core
    planes = blocks // PLANE
    half_planes = planes // 2
    spot = lax.rem(me, PLANE)
    level = me // PLANE
    bit_x, bit_y = lax.rem(spot, 2), spot // 2
    spot_x = spot + 1 - 2 * bit_x
    spot_y = spot + 2 - 4 * bit_y
    spot_d = spot_x + 2 - 4 * bit_y
    length, width = q_ref.shape
    heads = width // HEAD_DIM
    rows, cols = w_ref.shape
    half = rows // 2
    per_core = blocks // 2

    def at_seq(position):
        return (position, core)

    nbr_x = level * PLANE + spot_x
    nbr_y = level * PLANE + spot_y

    barrier = pltpu.get_barrier_semaphore()

    def greet(i, carry):
        pl.semaphore_signal(barrier, inc=1, device_id=at_seq(lax.rem(me + i, blocks)), device_id_type=MESH)
        return carry

    lax.fori_loop(1, blocks, greet, 0)
    pl.semaphore_signal(barrier, inc=1, device_id=(me, other), device_id_type=MESH)

    own_w = pltpu.make_async_copy(w_ref, w_all.at[me], local_sem.at[0])
    own_g = pltpu.make_async_copy(g_ref, g_all.at[core], local_sem.at[1])
    own_w.start()
    own_g.start()

    def head_cols(h):
        return pl.ds(pl.multiple_of(h * HEAD_DIM, HEAD_DIM), HEAD_DIM)

    def make_state(h, carry):
        c = head_cols(h)
        st_send[h] = contract_rows(k_ref[:, c], v_ref[:, c]).astype(jnp.bfloat16)
        return carry

    lax.fori_loop(0, heads, make_state, 0)
    st_recv[me] = st_send[me]

    pl.semaphore_wait(barrier, blocks)

    def leave(src, dst, kind, peer):
        @pl.when(peer != me)
        def _():
            pltpu.make_async_remote_copy(
                src_ref=src.at[peer], dst_ref=dst.at[me],
                send_sem=a_send_sem.at[kind, peer], recv_sem=a_recv_sem.at[kind, me],
                device_id=at_seq(peer), device_id_type=MESH,
            ).start()

    def exchange(src, dst, kind, start):
        def one(i, carry):
            peer = lax.rem(me + i, blocks)
            copy = pltpu.make_async_remote_copy(
                src_ref=src.at[peer], dst_ref=dst.at[me],
                send_sem=a_send_sem.at[kind, peer], recv_sem=a_recv_sem.at[kind, me],
                device_id=at_seq(peer), device_id_type=MESH,
            )
            if start:
                copy.start()
            else:
                copy.wait_send()
            return carry

        lax.fori_loop(1, blocks, one, 0)

    def arrived(src, dst, kind):
        def one(i, carry):
            peer = lax.rem(me + i, blocks)
            pltpu.make_async_remote_copy(
                src_ref=src.at[me], dst_ref=dst.at[peer],
                send_sem=a_send_sem.at[kind, me], recv_sem=a_recv_sem.at[kind, peer],
                device_id=at_seq(peer), device_id_type=MESH,
            ).wait_recv()
            return carry

        lax.fori_loop(1, blocks, one, 0)

    g_copy = pltpu.make_async_remote_copy(
        src_ref=g_ref, dst_ref=g_all.at[core], send_sem=g_sem.at[0], recv_sem=g_sem.at[1],
        device_id=(me, other), device_id_type=MESH,
    )
    g_copy.start()
    exchange(st_send, st_recv, 0, True)

    def piece(block, part, sems, target, own=False):
        span = pl.ds(part * half, half)
        return pltpu.make_async_remote_copy(
            src_ref=w_ref.at[span] if own else w_all.at[block, span],
            dst_ref=w_all.at[block, span],
            send_sem=sems.at[block, part], recv_sem=w_recv_sem.at[block, part],
            device_id=at_seq(target), device_id_type=MESH,
        )

    up_ok = level + 1 < planes
    down_ok = level > 0
    up = jnp.minimum(me + PLANE, blocks - PLANE + spot)
    down = jnp.maximum(me - PLANE, spot)

    for part in range(2):
        piece(me, part, wx_sem, nbr_x, True).start()
        piece(me, part, wy_sem, nbr_y, True).start()

        @pl.when(up_ok)
        def _():
            piece(me, part, wz_sem.at[0], up, True).start()

        @pl.when(down_ok)
        def _():
            piece(me, part, wz_sem.at[1], down, True).start()

    tables = visit_tables(planes)
    order = [pick([tables[z][k] for z in range(planes)], level) for k in range(planes)]

    def along_z(k, where, finish=False):
        plane = order[k]
        block = plane * PLANE + where
        going_up = plane < level
        for part in range(2):
            if not finish:
                piece(block, part, wx_sem, nbr_x).wait_recv()

            @pl.when(jnp.logical_and(going_up, up_ok))
            def _():
                copy = piece(block, part, wz_sem.at[0], up)
                copy.wait_send() if finish else copy.start()

            @pl.when(jnp.logical_and(jnp.logical_not(going_up), down_ok))
            def _():
                copy = piece(block, part, wz_sem.at[1], down)
                copy.wait_send() if finish else copy.start()

    def across(k, finish=False):
        block = order[k] * PLANE + spot
        for part in range(2):
            for copy in (piece(block, part, wx_sem, nbr_x), piece(block, part, wy_sem, nbr_y)):
                copy.wait_send() if finish else copy.start()

    def relay_step(k, finish=False):
        plane = order[k]
        to_x = piece(plane * PLANE + spot_y, 0, wx_sem, nbr_x)
        to_y = piece(plane * PLANE + spot_x, 1, wy_sem, nbr_y)
        for copy in (to_x, to_y):
            if finish:
                copy.wait_send()
            else:
                copy.wait_recv()
                copy.start()

    def cross_step(k, finish=False):
        block = order[k] * PLANE + spot_d
        for part in range(2):

            @pl.when(level == half_planes - 1)
            def _():
                copy = piece(block, part, wz_sem.at[0], up)
                copy.wait_send() if finish else copy.start()

            @pl.when(level == half_planes)
            def _():
                copy = piece(block, part, wz_sem.at[1], down)
                copy.wait_send() if finish else copy.start()

    def settle(k):
        plane = order[k]
        near = ((spot_y, 1), (spot_x, 0), (spot_d, 0), (spot_d, 1))
        far = ((spot_y, 0), (spot_x, 0), (spot_y, 1), (spot_x, 1))
        for where, part in near if k < half_planes else far:
            piece(plane * PLANE + where, part, wx_sem, nbr_x).wait_recv()

    causal = lower_mask(length)

    def score_step(h, carry):
        c = head_cols(h)
        kept = jnp.where(causal, contract_cols(q_ref[:, c], k_ref[:, c]), 0.0).astype(jnp.bfloat16)
        weights[h] = kept
        normed[h] = contract_mid(kept, v_ref[:, c])
        return carry

    def norm_step(h, carry):
        c = head_cols(h)
        numerator = normed[h] + contract_mid(q_ref[:, c], prefix[h])
        inv = 1.0 / jnp.sqrt(jnp.mean(numerator * numerator, axis=-1, keepdims=True) + 1e-06)
        value = numerator * inv
        normed[h] = value
        inv_spread[h] = jnp.broadcast_to(inv, (length, HEAD_DIM))
        attended[:, c] = value.astype(jnp.bfloat16)
        return carry

    tile = cols
    n_tiles = rows // tile

    def grad_cols(block):
        return g_all[block // per_core, :, pl.ds(pl.multiple_of(lax.rem(block, per_core) * cols, cols), cols)]

    def direction_step(k):
        base = order[k] * PLANE

        def one(n, carry):
            span = pl.ds(pl.multiple_of(n * tile, tile), tile)
            total = contract_cols(grad_cols(base), w_all[base, span])
            for s in range(1, PLANE):
                total = total + contract_cols(grad_cols(base + s), w_all[base + s, span])
            if k > 0:
                total = total + out_dir[:, span]
            out_dir[:, span] = total
            return carry

        lax.fori_loop(0, n_tiles, one, 0)

    def p_copy(slot):
        return pltpu.make_async_remote_copy(
            src_ref=p_send.at[slot], dst_ref=p_recv.at[slot],
            send_sem=p_send_sem.at[slot], recv_sem=p_recv_sem.at[slot],
            device_id=(me, other), device_id_type=MESH,
        )

    def partial_step(k):
        def one(s, carry):
            block = order[k] * PLANE + s
            term = contract_mid(attended[...], w_all[block]).astype(jnp.bfloat16)
            slot = lax.rem(block, per_core)

            @pl.when(block // per_core == core)
            def _():
                p_own[slot] = term

            @pl.when(block // per_core != core)
            def _():
                p_send[slot] = term
                p_copy(slot).start()

            return carry

        lax.fori_loop(0, PLANE, one, 0)

    lax.fori_loop(0, heads, score_step, 0)
    relay_step(0)
    along_z(1, spot)
    across(1)
    along_z(2, spot)
    arrived(st_send, st_recv, 0)

    def before_step(b, total):
        low = total.astype(jnp.bfloat16)
        pre_send[b] = low

        @pl.when(b == me)
        def _():
            prefix[me] = low

        return total + st_recv[b].astype(jnp.float32)

    lax.fori_loop(0, blocks, before_step, jnp.zeros((HEAD_DIM, HEAD_DIM), jnp.float32))
    exchange(pre_send, prefix, 1, True)

    settle(0)
    cross_step(0)
    relay_step(1)
    along_z(3, spot)
    across(2)
    own_w.wait()
    own_g.wait()
    g_copy.wait()
    direction_step(0)
    along_z(2, spot_d)
    settle(1)
    cross_step(1)
    across(3)
    direction_step(1)
    arrived(pre_send, prefix, 1)
    lax.fori_loop(0, heads, norm_step, 0)
    partial_step(0)
    along_z(3, spot_d)
    partial_step(1)
    settle(2)
    direction_step(2)
    partial_step(2)
    settle(3)
    direction_step(3)

    def numer_step(h, carry):
        c = head_cols(h)
        toward, unit = out_dir[:, c], normed[h]
        along = jnp.mean(toward * unit, axis=-1, keepdims=True)
        low = ((toward - unit * along) * inv_spread[h]).astype(jnp.bfloat16)
        ng[:, c] = low
        lg_send[h] = contract_rows(q_ref[:, c], low).astype(jnp.bfloat16)

        @pl.when(h > 0)
        def _():
            leave(lg_send, lg_recv, 2, h - 1)

        return carry

    lax.fori_loop(0, heads, numer_step, 0)
    leave(lg_send, lg_recv, 2, heads - 1)
    lg_recv[me] = lg_send[me]
    partial_step(planes - 1)
    arrived(lg_send, lg_recv, 2)

    def after_step(i, total):
        b = blocks - 1 - i
        low = total.astype(jnp.bfloat16)
        suf_send[b] = low

        @pl.when(b == me)
        def _():
            suffix[me] = low

        return total + lg_recv[b].astype(jnp.float32)

    lax.fori_loop(0, blocks, after_step, jnp.zeros((HEAD_DIM, HEAD_DIM), jnp.float32))
    exchange(suf_send, suffix, 3, True)

    def pair_step(h, carry):
        c = head_cols(h)
        low = ng[:, c]
        pair = jnp.where(causal, contract_cols(low, v_ref[:, c]), 0.0).astype(jnp.bfloat16)
        dq_ref[:, c] = (contract_mid(pair, k_ref[:, c]) + contract_cols(low, prefix[h])).astype(jnp.bfloat16)
        k_part[h] = contract_rows(pair, q_ref[:, c])
        v_part[h] = contract_rows(weights[h], low)
        return carry

    lax.fori_loop(0, heads, pair_step, 0)

    def mix_step(slot, carry):
        p_copy(slot).wait()
        c = pl.ds(pl.multiple_of(slot * cols, cols), cols)
        mixed_ref[:, c] = (p_own[slot].astype(jnp.float32) + p_recv[slot].astype(jnp.float32)).astype(jnp.bfloat16)
        return carry

    lax.fori_loop(0, per_core, mix_step, 0)
    arrived(suf_send, suffix, 3)

    def last_step(h, carry):
        c = head_cols(h)
        dk_ref[:, c] = (k_part[h] + contract_cols(v_ref[:, c], suffix[h])).astype(jnp.bfloat16)
        dv_ref[:, c] = (v_part[h] + contract_mid(k_ref[:, c], suffix[h])).astype(jnp.bfloat16)
        return carry

    lax.fori_loop(0, heads, last_step, 0)

    for part in range(2):
        piece(me, part, wx_sem, nbr_x, True).wait_send()
        piece(me, part, wy_sem, nbr_y, True).wait_send()

        @pl.when(up_ok)
        def _():
            piece(me, part, wz_sem.at[0], up, True).wait_send()

        @pl.when(down_ok)
        def _():
            piece(me, part, wz_sem.at[1], down, True).wait_send()

    for k in range(1, planes):
        along_z(k, spot, True)
        across(k, True)
    for k in range(half_planes):
        relay_step(k, True)
        cross_step(k, True)
    for k in range(half_planes, planes):
        along_z(k, spot_d, True)
    exchange(st_send, st_recv, 0, False)
    exchange(pre_send, prefix, 1, False)
    exchange(lg_send, lg_recv, 2, False)
    exchange(suf_send, suffix, 3, False)


def fused(blocks, queries, key_rows, values, out_weight, out_grad):
    length, width = queries.shape
    heads = width // HEAD_DIM
    rows, cols = out_weight.shape
    per_core = blocks // 2
    low, wide = jnp.bfloat16, jnp.float32
    state = pltpu.VMEM((blocks, HEAD_DIM, HEAD_DIM), low)
    by_head = pltpu.VMEM((heads, length, HEAD_DIM), wide)
    flat = pltpu.VMEM((length, width), low)
    parts = pltpu.VMEM((per_core, length, cols), low)
    dma = pltpu.SemaphoreType.DMA
    out = jax.ShapeDtypeStruct((length, width), low)
    vmem, anywhere = pl.BlockSpec(memory_space=pltpu.VMEM), pl.BlockSpec(memory_space=pl.ANY)
    return pl.pallas_call(
        functools.partial(kernel, blocks),
        out_shape=(out, out, out, out),
        in_specs=[vmem, vmem, vmem, anywhere, anywhere],
        out_specs=(vmem, vmem, vmem, vmem),
        scratch_shapes=[
            pltpu.VMEM((blocks, rows, cols), low),
            pltpu.VMEM((2, length, width), low),
            state, state, state, state, state, state, state, state,
            pltpu.VMEM((length, rows), wide),
            by_head, by_head,
            pltpu.VMEM((heads, length, length), low),
            flat, parts, parts, parts, flat, by_head, by_head,
            dma((blocks, 2)), dma((blocks, 2)), dma((blocks, 2)), dma((2, blocks, 2)),
            dma((2,)), dma((2,)), dma((4, blocks)), dma((4, blocks)), dma((per_core,)), dma((per_core,)),
        ],
        compiler_params=pltpu.CompilerParams(
            collective_id=0, has_side_effects=True, vmem_limit_bytes=60 * 2**20
        ),
    )(queries, key_rows, values, out_weight, out_grad)


def solution(mesh):
    blocks, cores = mesh.shape["seq"], mesh.shape["head"]

    def step(queries, key_rows, values, out_weight, out_grad):
        heads = queries.shape[1] // HEAD_DIM
        fits = cores == 2 and blocks == PLANE * PLANE and heads == blocks and out_weight.shape[1] % HEAD_DIM == 0
        fits = fits and out_weight.shape[0] == queries.shape[1] and out_weight.shape[0] % out_weight.shape[1] == 0
        if fits and out_weight.shape[1] * blocks == queries.shape[1] * cores:
            return fused(blocks, queries, key_rows, values, out_weight, out_grad)
        return per_device(queries, key_rows, values, out_weight, out_grad)

    placed = (
        P("seq", "head"),
        P("seq", "head"),
        P("seq", "head"),
        P("head", "seq"),
        P("seq", "head"),
    )
    return jax.shard_map(
        step,
        mesh=mesh,
        in_specs=placed,
        out_specs=(P("seq", "head"), P("seq", "head"), P("seq", "head"), P("seq", "head")),
        check_vma=False,
    )
```

```python
import functools

import jax
import jax.numpy as jnp
from jax import lax
from jax.experimental import pallas as pl
from jax.experimental.pallas import tpu as pltpu
from jax.sharding import PartitionSpec as P

HEAD_DIM = 128
MESH = pl.DeviceIdType.MESH
PLANE = 4


def prefix_2(value, axis, combine, identity):
    length, position = (lax.axis_size(axis), lax.axis_index(axis))
    everything = lax.all_gather(value, axis)
    start = jnp.broadcast_to(jnp.asarray(identity, value.dtype), value.shape)

    def hop(k, before):
        reached = k < position
        new = combine(before, everything[k])
        return jnp.where(reached, new, before)

    return lax.fori_loop(0, length, hop, start)


def prefix_3(value, axis, combine, identity):
    length, position = (lax.axis_size(axis), lax.axis_index(axis))
    everything = lax.all_gather(value.astype(jnp.bfloat16), axis)
    start = jnp.broadcast_to(jnp.asarray(identity, value.dtype), value.shape)

    def hop(k, before):
        at = length - 1 - k
        reached = at > position
        new = combine(before, everything[at].astype(value.dtype))
        return jnp.where(reached, new, before)

    return lax.fori_loop(0, length, hop, start)


def lower_mask(length):
    row_ids = lax.broadcasted_iota(jnp.int32, (length, length), 0)
    col_ids = lax.broadcasted_iota(jnp.int32, (length, length), 1)
    return row_ids >= col_ids


def add_states(earlier, latter):
    return earlier + latter


def contract_cols(left_side, right_side):
    return lax.dot_general(
        left_side, right_side, (((1,), (1,)), ((), ())), preferred_element_type=jnp.float32
    )


def contract_rows(left_side, right_side):
    return lax.dot_general(
        left_side, right_side, (((0,), (0,)), ((), ())), preferred_element_type=jnp.float32
    )


def contract_mid(left_side, right_side):
    return jnp.dot(left_side, right_side, preferred_element_type=jnp.float32)


def per_device(queries, key_rows, values, out_weight, out_grad):
    length = queries.shape[0]
    heads_here = queries.shape[1] // HEAD_DIM
    query_heads = queries.reshape(length, heads_here, HEAD_DIM)
    key_heads = key_rows.reshape(length, heads_here, HEAD_DIM)
    value_heads = values.reshape(length, heads_here, HEAD_DIM)
    causal = lower_mask(length)[None]
    local_state = jnp.einsum(
        "shd,she->hde", key_heads, value_heads, preferred_element_type=jnp.float32
    )
    prefix = prefix_2(local_state, "seq", add_states, jnp.zeros_like(local_state))
    prefix_low = prefix.astype(jnp.bfloat16)
    scores = jnp.einsum("thd,shd->hts", query_heads, key_heads, preferred_element_type=jnp.float32)
    weights = jnp.where(causal, scores, 0.0).astype(jnp.bfloat16)
    numerator = jnp.einsum("hts,she->the", weights, value_heads, preferred_element_type=jnp.float32)
    numerator = numerator + jnp.einsum(
        "thd,hde->the", query_heads, prefix_low, preferred_element_type=jnp.float32
    )
    spread = jnp.sqrt(jnp.mean(numerator * numerator, axis=-1, keepdims=True) + 1e-06)
    normed = numerator / spread
    attended = normed.astype(jnp.bfloat16).reshape(length, heads_here * HEAD_DIM)
    full_weight = lax.all_gather(out_weight, "seq", axis=1, tiled=True)
    partial_value = jnp.dot(attended, full_weight, preferred_element_type=jnp.float32)
    layer_out = lax.psum_scatter(
        partial_value.astype(jnp.bfloat16), "head", scatter_dimension=1, tiled=True
    )
    out_dir = contract_cols(lax.all_gather(out_grad, "head", axis=1, tiled=True), full_weight)
    out_dir = out_dir.reshape(length, heads_here, HEAD_DIM)
    along_dir = jnp.mean(out_dir * normed, axis=-1, keepdims=True)
    numer_grad = ((out_dir - normed * along_dir) / spread).astype(jnp.bfloat16)
    local_grad = jnp.einsum(
        "thd,the->hde", query_heads, numer_grad, preferred_element_type=jnp.float32
    )
    suffix = prefix_3(local_grad, "seq", add_states, jnp.zeros_like(local_grad))
    suffix_low = suffix.astype(jnp.bfloat16)
    pair_scores = jnp.einsum(
        "the,she->hts", numer_grad, value_heads, preferred_element_type=jnp.float32
    )
    pair_low = jnp.where(causal, pair_scores, 0.0).astype(jnp.bfloat16)
    query_out = jnp.einsum("hts,shd->thd", pair_low, key_heads, preferred_element_type=jnp.float32)
    query_out = query_out + jnp.einsum(
        "the,hde->thd", numer_grad, prefix_low, preferred_element_type=jnp.float32
    )
    key_out = jnp.einsum("hts,thd->shd", pair_low, query_heads, preferred_element_type=jnp.float32)
    key_out = key_out + jnp.einsum(
        "she,hde->shd", value_heads, suffix_low, preferred_element_type=jnp.float32
    )
    value_out = jnp.einsum("hts,the->she", weights, numer_grad, preferred_element_type=jnp.float32)
    value_out = value_out + jnp.einsum(
        "shd,hde->she", key_heads, suffix_low, preferred_element_type=jnp.float32
    )
    flat_shape = (length, heads_here * HEAD_DIM)
    return (
        layer_out,
        query_out.reshape(flat_shape).astype(jnp.bfloat16),
        key_out.reshape(flat_shape).astype(jnp.bfloat16),
        value_out.reshape(flat_shape).astype(jnp.bfloat16),
    )


def visit_tables(planes):
    half, rows = planes // 2, []
    for own in range(planes):
        rows.append(sorted(range(planes), key=lambda other: (other // half != own // half, abs(other - own))))
    return rows


def pick(table, position):
    found = jnp.int32(table[0])
    for at in range(1, len(table)):
        found = jnp.where(position == at, jnp.int32(table[at]), found)
    return found


def kernel(
    blocks, q_in, k_in, v_in, w_ref, g_ref,
    mixed_ref, dq_ref, dk_ref, dv_ref,
    q_ref, k_ref, v_ref, w_all, g_all, st_send, st_recv, pre_send, prefix, lg_send, lg_recv, suf_send, suffix,
    out_dir, normed, inv_spread, weights, attended, p_own, p_send, p_recv, ng, k_part, v_part,
    w_recv_sem, wx_sem, wy_sem, wz_sem, local_sem, g_sem, a_send_sem, a_recv_sem, p_send_sem, p_recv_sem,
):
    me = lax.axis_index("seq")
    core = lax.axis_index("head")
    other = 1 - core
    planes = blocks // PLANE
    half_planes = planes // 2
    spot = lax.rem(me, PLANE)
    level = me // PLANE
    bit_x, bit_y = lax.rem(spot, 2), spot // 2
    spot_x = spot + 1 - 2 * bit_x
    spot_y = spot + 2 - 4 * bit_y
    spot_d = spot_x + 2 - 4 * bit_y
    length, width = q_ref.shape
    heads = width // HEAD_DIM
    rows, cols = w_ref.shape
    half = rows // 2
    per_core = blocks // 2

    def at_seq(position):
        return (position, core)

    nbr_x = level * PLANE + spot_x
    nbr_y = level * PLANE + spot_y

    q_load = pltpu.make_async_copy(q_in, q_ref, local_sem.at[2])
    k_load = pltpu.make_async_copy(k_in, k_ref, local_sem.at[3])
    v_load = pltpu.make_async_copy(v_in, v_ref, local_sem.at[4])
    k_load.start()
    v_load.start()
    barrier = pltpu.get_barrier_semaphore()

    def greet(i, carry):
        pl.semaphore_signal(barrier, inc=1, device_id=at_seq(lax.rem(me + i, blocks)), device_id_type=MESH)
        return carry

    lax.fori_loop(1, blocks, greet, 0)
    pl.semaphore_signal(barrier, inc=1, device_id=(me, other), device_id_type=MESH)

    own_w = pltpu.make_async_copy(w_ref, w_all.at[me], local_sem.at[0])
    own_g = pltpu.make_async_copy(g_ref, g_all.at[core], local_sem.at[1])
    q_load.start()
    own_w.start()
    own_g.start()
    k_load.wait()
    v_load.wait()

    def head_cols(h):
        return pl.ds(pl.multiple_of(h * HEAD_DIM, HEAD_DIM), HEAD_DIM)

    def make_state(h, carry):
        c = head_cols(h)
        st_send[h] = contract_rows(k_ref[:, c], v_ref[:, c]).astype(jnp.bfloat16)
        return carry

    lax.fori_loop(0, heads, make_state, 0)
    st_recv[me] = st_send[me]

    pl.semaphore_wait(barrier, blocks)

    def leave(src, dst, kind, peer):
        @pl.when(peer != me)
        def _():
            pltpu.make_async_remote_copy(
                src_ref=src.at[peer], dst_ref=dst.at[me],
                send_sem=a_send_sem.at[kind, peer], recv_sem=a_recv_sem.at[kind, me],
                device_id=at_seq(peer), device_id_type=MESH,
            ).start()

    def exchange(src, dst, kind, start):
        def one(i, carry):
            peer = lax.rem(me + i, blocks)
            copy = pltpu.make_async_remote_copy(
                src_ref=src.at[peer], dst_ref=dst.at[me],
                send_sem=a_send_sem.at[kind, peer], recv_sem=a_recv_sem.at[kind, me],
                device_id=at_seq(peer), device_id_type=MESH,
            )
            if start:
                copy.start()
            else:
                copy.wait_send()
            return carry

        lax.fori_loop(1, blocks, one, 0)

    def arrived(src, dst, kind):
        def one(i, carry):
            peer = lax.rem(me + i, blocks)
            pltpu.make_async_remote_copy(
                src_ref=src.at[me], dst_ref=dst.at[peer],
                send_sem=a_send_sem.at[kind, me], recv_sem=a_recv_sem.at[kind, peer],
                device_id=at_seq(peer), device_id_type=MESH,
            ).wait_recv()
            return carry

        lax.fori_loop(1, blocks, one, 0)

    g_copy = pltpu.make_async_remote_copy(
        src_ref=g_ref, dst_ref=g_all.at[core], send_sem=g_sem.at[0], recv_sem=g_sem.at[1],
        device_id=(me, other), device_id_type=MESH,
    )
    g_copy.start()
    exchange(st_send, st_recv, 0, True)

    def piece(block, part, sems, target, own=False):
        span = pl.ds(part * half, half)
        return pltpu.make_async_remote_copy(
            src_ref=w_ref.at[span] if own else w_all.at[block, span],
            dst_ref=w_all.at[block, span],
            send_sem=sems.at[block, part], recv_sem=w_recv_sem.at[block, part],
            device_id=at_seq(target), device_id_type=MESH,
        )

    up_ok = level + 1 < planes
    down_ok = level > 0
    up = jnp.minimum(me + PLANE, blocks - PLANE + spot)
    down = jnp.maximum(me - PLANE, spot)

    for part in range(2):
        piece(me, part, wx_sem, nbr_x, True).start()
        piece(me, part, wy_sem, nbr_y, True).start()

        @pl.when(up_ok)
        def _():
            piece(me, part, wz_sem.at[0], up, True).start()

        @pl.when(down_ok)
        def _():
            piece(me, part, wz_sem.at[1], down, True).start()

    tables = visit_tables(planes)
    order = [pick([tables[z][k] for z in range(planes)], level) for k in range(planes)]

    def passing(k):
        return jnp.where(order[k] < level, up_ok, down_ok)

    def along_z(k, where, finish=False):
        plane = order[k]
        block = plane * PLANE + where
        going_up = plane < level
        for part in range(2):
            for sems, way, go in ((wz_sem.at[0], up, going_up), (wz_sem.at[1], down, jnp.logical_not(going_up))):

                @pl.when(jnp.logical_and(go, passing(k)))
                def _():
                    copy = piece(block, part, sems, way)
                    if finish:
                        copy.wait_send()
                    else:
                        copy.wait_recv()
                        copy.start()

    def end_of_z(k, where, part):
        @pl.when(jnp.logical_not(passing(k)))
        def _():
            piece(order[k] * PLANE + where, part, wx_sem, nbr_x).wait_recv()

    def across(k, finish=False):
        block = order[k] * PLANE + spot
        for part in range(2):
            if not finish:
                end_of_z(k, spot, part)
            for copy in (piece(block, part, wx_sem, nbr_x), piece(block, part, wy_sem, nbr_y)):
                copy.wait_send() if finish else copy.start()

    def relay_step(k, finish=False):
        plane = order[k]
        to_x = piece(plane * PLANE + spot_y, 0, wx_sem, nbr_x)
        to_y = piece(plane * PLANE + spot_x, 1, wy_sem, nbr_y)
        for copy in (to_x, to_y):
            if finish:
                copy.wait_send()
            else:
                copy.wait_recv()
                copy.start()

    def cross_step(k, finish=False):
        block = order[k] * PLANE + spot_d
        for part in range(2):

            @pl.when(level == half_planes - 1)
            def _():
                copy = piece(block, part, wz_sem.at[0], up)
                copy.wait_send() if finish else copy.start()

            @pl.when(level == half_planes)
            def _():
                copy = piece(block, part, wz_sem.at[1], down)
                copy.wait_send() if finish else copy.start()

    def settle(k):
        plane = order[k]
        near = ((spot_y, 1), (spot_x, 0), (spot_d, 0), (spot_d, 1))
        far = ((spot_y, 0), (spot_x, 0), (spot_y, 1), (spot_x, 1))
        for where, part in near if k < half_planes else far:
            piece(plane * PLANE + where, part, wx_sem, nbr_x).wait_recv()
        if k >= half_planes:
            for part in range(2):
                end_of_z(k, spot_d, part)

    causal = lower_mask(length)

    def score_step(h, carry):
        c = head_cols(h)
        kept = jnp.where(causal, contract_cols(q_ref[:, c], k_ref[:, c]), 0.0).astype(jnp.bfloat16)
        weights[h] = kept
        normed[h] = contract_mid(kept, v_ref[:, c])
        return carry

    def norm_step(h, carry):
        c = head_cols(h)
        numerator = normed[h] + contract_mid(q_ref[:, c], prefix[h])
        inv = 1.0 / jnp.sqrt(jnp.mean(numerator * numerator, axis=-1, keepdims=True) + 1e-06)
        value = numerator * inv
        normed[h] = value
        inv_spread[h] = jnp.broadcast_to(inv, (length, HEAD_DIM))
        attended[:, c] = value.astype(jnp.bfloat16)
        return carry

    tile = cols
    n_tiles = rows // tile

    def grad_cols(block):
        return g_all[block // per_core, :, pl.ds(pl.multiple_of(lax.rem(block, per_core) * cols, cols), cols)]

    def direction_step(k):
        base = order[k] * PLANE

        def one(n, carry):
            span = pl.ds(pl.multiple_of(n * tile, tile), tile)
            total = contract_cols(grad_cols(base), w_all[base, span])
            for s in range(1, PLANE):
                total = total + contract_cols(grad_cols(base + s), w_all[base + s, span])
            if k > 0:
                total = total + out_dir[:, span]
            out_dir[:, span] = total
            return carry

        lax.fori_loop(0, n_tiles, one, 0)

    def p_copy(slot):
        return pltpu.make_async_remote_copy(
            src_ref=p_send.at[slot], dst_ref=p_recv.at[slot],
            send_sem=p_send_sem.at[slot], recv_sem=p_recv_sem.at[slot],
            device_id=(me, other), device_id_type=MESH,
        )

    def partial_step(k):
        def one(s, carry):
            block = order[k] * PLANE + s
            term = contract_mid(attended[...], w_all[block]).astype(jnp.bfloat16)
            slot = lax.rem(block, per_core)

            @pl.when(block // per_core == core)
            def _():
                p_own[slot] = term

            @pl.when(block // per_core != core)
            def _():
                p_send[slot] = term
                p_copy(slot).start()

            return carry

        lax.fori_loop(0, PLANE, one, 0)

    q_load.wait()
    lax.fori_loop(0, heads, score_step, 0)
    relay_step(0)
    along_z(1, spot)
    across(1)
    along_z(2, spot)
    arrived(st_send, st_recv, 0)

    def before_step(b, total):
        low = total.astype(jnp.bfloat16)
        pre_send[b] = low

        @pl.when(b == me)
        def _():
            prefix[me] = low

        return total + st_recv[b].astype(jnp.float32)

    lax.fori_loop(0, blocks, before_step, jnp.zeros((HEAD_DIM, HEAD_DIM), jnp.float32))
    exchange(pre_send, prefix, 1, True)

    settle(0)
    cross_step(0)
    along_z(3, spot)
    relay_step(1)
    across(2)
    own_w.wait()
    own_g.wait()
    g_copy.wait()
    direction_step(0)
    along_z(2, spot_d)
    settle(1)
    cross_step(1)
    across(3)
    direction_step(1)
    arrived(pre_send, prefix, 1)
    lax.fori_loop(0, heads, norm_step, 0)
    partial_step(0)
    along_z(3, spot_d)
    partial_step(1)
    settle(2)
    direction_step(2)
    partial_step(2)
    settle(3)
    direction_step(3)

    def numer_step(h, carry):
        c = head_cols(h)
        toward, unit = out_dir[:, c], normed[h]
        along = jnp.mean(toward * unit, axis=-1, keepdims=True)
        low = ((toward - unit * along) * inv_spread[h]).astype(jnp.bfloat16)
        ng[:, c] = low
        lg_send[h] = contract_rows(q_ref[:, c], low).astype(jnp.bfloat16)

        @pl.when(h > 0)
        def _():
            leave(lg_send, lg_recv, 2, h - 1)

        return carry

    lax.fori_loop(0, heads, numer_step, 0)
    leave(lg_send, lg_recv, 2, heads - 1)
    lg_recv[me] = lg_send[me]
    partial_step(planes - 1)
    arrived(lg_send, lg_recv, 2)

    def after_step(i, total):
        b = blocks - 1 - i
        low = total.astype(jnp.bfloat16)
        suf_send[b] = low

        @pl.when(b == me)
        def _():
            suffix[me] = low

        return total + lg_recv[b].astype(jnp.float32)

    lax.fori_loop(0, blocks, after_step, jnp.zeros((HEAD_DIM, HEAD_DIM), jnp.float32))
    exchange(suf_send, suffix, 3, True)

    def pair_step(h, carry):
        c = head_cols(h)
        low = ng[:, c]
        pair = jnp.where(causal, contract_cols(low, v_ref[:, c]), 0.0).astype(jnp.bfloat16)
        dq_ref[:, c] = (contract_mid(pair, k_ref[:, c]) + contract_cols(low, prefix[h])).astype(jnp.bfloat16)
        k_part[h] = contract_rows(pair, q_ref[:, c])
        v_part[h] = contract_rows(weights[h], low)
        return carry

    lax.fori_loop(0, heads, pair_step, 0)

    def mix_step(slot, carry):
        p_copy(slot).wait()
        c = pl.ds(pl.multiple_of(slot * cols, cols), cols)
        mixed_ref[:, c] = (p_own[slot].astype(jnp.float32) + p_recv[slot].astype(jnp.float32)).astype(jnp.bfloat16)
        return carry

    lax.fori_loop(0, per_core, mix_step, 0)
    arrived(suf_send, suffix, 3)

    def last_step(h, carry):
        c = head_cols(h)
        dk_ref[:, c] = (k_part[h] + contract_cols(v_ref[:, c], suffix[h])).astype(jnp.bfloat16)
        dv_ref[:, c] = (v_part[h] + contract_mid(k_ref[:, c], suffix[h])).astype(jnp.bfloat16)
        return carry

    lax.fori_loop(0, heads, last_step, 0)

    for part in range(2):
        piece(me, part, wx_sem, nbr_x, True).wait_send()
        piece(me, part, wy_sem, nbr_y, True).wait_send()

        @pl.when(up_ok)
        def _():
            piece(me, part, wz_sem.at[0], up, True).wait_send()

        @pl.when(down_ok)
        def _():
            piece(me, part, wz_sem.at[1], down, True).wait_send()

    for k in range(1, planes):
        along_z(k, spot, True)
        across(k, True)
    for k in range(half_planes):
        relay_step(k, True)
        cross_step(k, True)
    for k in range(half_planes, planes):
        along_z(k, spot_d, True)
    exchange(st_send, st_recv, 0, False)
    exchange(pre_send, prefix, 1, False)
    exchange(lg_send, lg_recv, 2, False)
    exchange(suf_send, suffix, 3, False)


def store_kernel(*refs):
    count = (len(refs) - 1) // 2
    copies = [pltpu.make_async_copy(refs[i], refs[count + i], refs[-1].at[i]) for i in range(count)]
    for copy in copies:
        copy.start()
    for copy in copies:
        copy.wait()


def store(*arrays):
    count = len(arrays)
    return pl.pallas_call(
        store_kernel,
        out_shape=tuple(jax.ShapeDtypeStruct(a.shape, a.dtype) for a in arrays),
        in_specs=[pl.BlockSpec(memory_space=pltpu.VMEM)] * count,
        out_specs=(pl.BlockSpec(memory_space=pltpu.HBM),) * count,
        scratch_shapes=[pltpu.SemaphoreType.DMA((count,))],
        compiler_params=pltpu.CompilerParams(vmem_limit_bytes=8 * 2**20),
    )(*arrays)


def fused(blocks, queries, key_rows, values, out_weight, out_grad):
    length, width = queries.shape
    heads = width // HEAD_DIM
    rows, cols = out_weight.shape
    per_core = blocks // 2
    low, wide = jnp.bfloat16, jnp.float32
    state = pltpu.VMEM((blocks, HEAD_DIM, HEAD_DIM), low)
    by_head = pltpu.VMEM((heads, length, HEAD_DIM), wide)
    flat = pltpu.VMEM((length, width), low)
    parts = pltpu.VMEM((per_core, length, cols), low)
    dma = pltpu.SemaphoreType.DMA
    out = jax.ShapeDtypeStruct((length, width), low)
    vmem, in_hbm = pl.BlockSpec(memory_space=pltpu.VMEM), pl.BlockSpec(memory_space=pltpu.HBM)
    results = pl.pallas_call(
        functools.partial(kernel, blocks),
        out_shape=(out, out, out, out),
        in_specs=[in_hbm] * 5,
        out_specs=(vmem, vmem, vmem, vmem),
        scratch_shapes=[
            flat, flat, flat,
            pltpu.VMEM((blocks, rows, cols), low),
            pltpu.VMEM((2, length, width), low),
            state, state, state, state, state, state, state, state,
            pltpu.VMEM((length, rows), wide),
            by_head, by_head,
            pltpu.VMEM((heads, length, length), low),
            flat, parts, parts, parts, flat, by_head, by_head,
            dma((blocks, 2)), dma((blocks, 2)), dma((blocks, 2)), dma((2, blocks, 2)),
            dma((5,)), dma((2,)), dma((4, blocks)), dma((4, blocks)), dma((per_core,)), dma((per_core,)),
        ],
        compiler_params=pltpu.CompilerParams(
            collective_id=0, has_side_effects=True, vmem_limit_bytes=46 * 2**20
        ),
    )(queries, key_rows, values, out_weight, out_grad)
    return store(*results)


def solution(mesh):
    blocks, cores = mesh.shape["seq"], mesh.shape["head"]

    def step(queries, key_rows, values, out_weight, out_grad):
        heads = queries.shape[1] // HEAD_DIM
        fits = cores == 2 and blocks == PLANE * PLANE and heads == blocks and out_weight.shape[1] % HEAD_DIM == 0
        fits = fits and out_weight.shape[0] == queries.shape[1] and out_weight.shape[0] % out_weight.shape[1] == 0
        if fits and out_weight.shape[1] * blocks == queries.shape[1] * cores:
            return fused(blocks, queries, key_rows, values, out_weight, out_grad)
        return per_device(queries, key_rows, values, out_weight, out_grad)

    placed = (
        P("seq", "head"),
        P("seq", "head"),
        P("seq", "head"),
        P("head", "seq"),
        P("seq", "head"),
    )
    return jax.shard_map(
        step,
        mesh=mesh,
        in_specs=placed,
        out_specs=(P("seq", "head"), P("seq", "head"), P("seq", "head"), P("seq", "head")),
        check_vma=False,
    )
```

```python
import functools

import jax
import jax.numpy as jnp
from jax import lax
from jax.experimental import pallas as pl
from jax.experimental.pallas import tpu as pltpu
from jax.sharding import PartitionSpec as P

HEAD_DIM = 128
MESH = pl.DeviceIdType.MESH
PLANE = 4


def prefix_2(value, axis, combine, identity):
    length, position = (lax.axis_size(axis), lax.axis_index(axis))
    everything = lax.all_gather(value, axis)
    start = jnp.broadcast_to(jnp.asarray(identity, value.dtype), value.shape)

    def hop(k, before):
        reached = k < position
        new = combine(before, everything[k])
        return jnp.where(reached, new, before)

    return lax.fori_loop(0, length, hop, start)


def prefix_3(value, axis, combine, identity):
    length, position = (lax.axis_size(axis), lax.axis_index(axis))
    everything = lax.all_gather(value.astype(jnp.bfloat16), axis)
    start = jnp.broadcast_to(jnp.asarray(identity, value.dtype), value.shape)

    def hop(k, before):
        at = length - 1 - k
        reached = at > position
        new = combine(before, everything[at].astype(value.dtype))
        return jnp.where(reached, new, before)

    return lax.fori_loop(0, length, hop, start)


def lower_mask(length):
    row_ids = lax.broadcasted_iota(jnp.int32, (length, length), 0)
    col_ids = lax.broadcasted_iota(jnp.int32, (length, length), 1)
    return row_ids >= col_ids


def add_states(earlier, latter):
    return earlier + latter


def contract_cols(left_side, right_side):
    return lax.dot_general(
        left_side, right_side, (((1,), (1,)), ((), ())), preferred_element_type=jnp.float32
    )


def contract_rows(left_side, right_side):
    return lax.dot_general(
        left_side, right_side, (((0,), (0,)), ((), ())), preferred_element_type=jnp.float32
    )


def contract_mid(left_side, right_side):
    return jnp.dot(left_side, right_side, preferred_element_type=jnp.float32)


def per_device(queries, key_rows, values, out_weight, out_grad):
    length = queries.shape[0]
    heads_here = queries.shape[1] // HEAD_DIM
    query_heads = queries.reshape(length, heads_here, HEAD_DIM)
    key_heads = key_rows.reshape(length, heads_here, HEAD_DIM)
    value_heads = values.reshape(length, heads_here, HEAD_DIM)
    causal = lower_mask(length)[None]
    local_state = jnp.einsum(
        "shd,she->hde", key_heads, value_heads, preferred_element_type=jnp.float32
    )
    prefix = prefix_2(local_state, "seq", add_states, jnp.zeros_like(local_state))
    prefix_low = prefix.astype(jnp.bfloat16)
    scores = jnp.einsum("thd,shd->hts", query_heads, key_heads, preferred_element_type=jnp.float32)
    weights = jnp.where(causal, scores, 0.0).astype(jnp.bfloat16)
    numerator = jnp.einsum("hts,she->the", weights, value_heads, preferred_element_type=jnp.float32)
    numerator = numerator + jnp.einsum(
        "thd,hde->the", query_heads, prefix_low, preferred_element_type=jnp.float32
    )
    spread = jnp.sqrt(jnp.mean(numerator * numerator, axis=-1, keepdims=True) + 1e-06)
    normed = numerator / spread
    attended = normed.astype(jnp.bfloat16).reshape(length, heads_here * HEAD_DIM)
    full_weight = lax.all_gather(out_weight, "seq", axis=1, tiled=True)
    partial_value = jnp.dot(attended, full_weight, preferred_element_type=jnp.float32)
    layer_out = lax.psum_scatter(
        partial_value.astype(jnp.bfloat16), "head", scatter_dimension=1, tiled=True
    )
    out_dir = contract_cols(lax.all_gather(out_grad, "head", axis=1, tiled=True), full_weight)
    out_dir = out_dir.reshape(length, heads_here, HEAD_DIM)
    along_dir = jnp.mean(out_dir * normed, axis=-1, keepdims=True)
    numer_grad = ((out_dir - normed * along_dir) / spread).astype(jnp.bfloat16)
    local_grad = jnp.einsum(
        "thd,the->hde", query_heads, numer_grad, preferred_element_type=jnp.float32
    )
    suffix = prefix_3(local_grad, "seq", add_states, jnp.zeros_like(local_grad))
    suffix_low = suffix.astype(jnp.bfloat16)
    pair_scores = jnp.einsum(
        "the,she->hts", numer_grad, value_heads, preferred_element_type=jnp.float32
    )
    pair_low = jnp.where(causal, pair_scores, 0.0).astype(jnp.bfloat16)
    query_out = jnp.einsum("hts,shd->thd", pair_low, key_heads, preferred_element_type=jnp.float32)
    query_out = query_out + jnp.einsum(
        "the,hde->thd", numer_grad, prefix_low, preferred_element_type=jnp.float32
    )
    key_out = jnp.einsum("hts,thd->shd", pair_low, query_heads, preferred_element_type=jnp.float32)
    key_out = key_out + jnp.einsum(
        "she,hde->shd", value_heads, suffix_low, preferred_element_type=jnp.float32
    )
    value_out = jnp.einsum("hts,the->she", weights, numer_grad, preferred_element_type=jnp.float32)
    value_out = value_out + jnp.einsum(
        "shd,hde->she", key_heads, suffix_low, preferred_element_type=jnp.float32
    )
    flat_shape = (length, heads_here * HEAD_DIM)
    return (
        layer_out,
        query_out.reshape(flat_shape).astype(jnp.bfloat16),
        key_out.reshape(flat_shape).astype(jnp.bfloat16),
        value_out.reshape(flat_shape).astype(jnp.bfloat16),
    )


def visit_tables(planes):
    half, rows = planes // 2, []
    for own in range(planes):
        rows.append(sorted(range(planes), key=lambda other: (other // half != own // half, abs(other - own))))
    return rows


def pick(table, position):
    found = jnp.int32(table[0])
    for at in range(1, len(table)):
        found = jnp.where(position == at, jnp.int32(table[at]), found)
    return found


def kernel(
    blocks, q_in, k_in, v_in, w_ref, g_ref,
    mixed_ref, dq_ref, dk_ref, dv_ref,
    q_ref, k_ref, v_ref, w_all, g_all, st_send, st_recv, pre_send, prefix, lg_send, lg_recv, suf_send, suffix,
    out_dir, normed, inv_spread, weights, attended, p_own, p_send, p_recv, ng, k_part, v_part,
    x_send, x_recv,
    w_recv_sem, wx_sem, wy_sem, wz_sem, local_sem, g_sem, a_send_sem, a_recv_sem, p_send_sem, p_recv_sem,
    x_send_sem, x_recv_sem,
):
    me = lax.axis_index("seq")
    core = lax.axis_index("head")
    other = 1 - core
    planes = blocks // PLANE
    half_planes = planes // 2
    size = blocks // 2
    share = st_send.shape[0] // size
    team, rank = me // size, lax.rem(me, size)
    spot = lax.rem(me, PLANE)
    level = me // PLANE
    bit_x, bit_y = lax.rem(spot, 2), spot // 2
    spot_x = spot + 1 - 2 * bit_x
    spot_y = spot + 2 - 4 * bit_y
    spot_d = spot_x + 2 - 4 * bit_y
    length, width = q_ref.shape
    heads = width // HEAD_DIM
    rows, cols = w_ref.shape
    half = rows // 2
    per_core = blocks // 2

    def at_seq(position):
        return (position, core)

    nbr_x = level * PLANE + spot_x
    nbr_y = level * PLANE + spot_y

    q_load = pltpu.make_async_copy(q_in, q_ref, local_sem.at[2])
    k_load = pltpu.make_async_copy(k_in, k_ref, local_sem.at[3])
    v_load = pltpu.make_async_copy(v_in, v_ref, local_sem.at[4])
    k_load.start()
    v_load.start()
    barrier = pltpu.get_barrier_semaphore()

    def greet(i, carry):
        pl.semaphore_signal(barrier, inc=1, device_id=at_seq(lax.rem(me + i, blocks)), device_id_type=MESH)
        return carry

    lax.fori_loop(1, blocks, greet, 0)
    pl.semaphore_signal(barrier, inc=1, device_id=(me, other), device_id_type=MESH)

    own_w = pltpu.make_async_copy(w_ref, w_all.at[me], local_sem.at[0])
    own_g = pltpu.make_async_copy(g_ref, g_all.at[core], local_sem.at[1])
    q_load.start()
    own_w.start()
    own_g.start()
    k_load.wait()
    v_load.wait()

    def head_cols(h):
        return pl.ds(pl.multiple_of(h * HEAD_DIM, HEAD_DIM), HEAD_DIM)

    def make_state(h, carry):
        c = head_cols(h)
        st_send[h] = contract_rows(k_ref[:, c], v_ref[:, c]).astype(jnp.bfloat16)
        return carry

    lax.fori_loop(0, heads, make_state, 0)
    st_recv[rank] = st_send[pl.ds(rank * share, share)]

    pl.semaphore_wait(barrier, blocks)

    def state_copy(src, dst, kind, peer):
        return pltpu.make_async_remote_copy(
            src_ref=src(peer), dst_ref=dst(rank),
            send_sem=a_send_sem.at[kind, peer], recv_sem=a_recv_sem.at[kind, rank],
            device_id=at_seq(team * size + peer), device_id_type=MESH,
        )

    def leave(src, dst, kind, peer):
        @pl.when(peer != rank)
        def _():
            state_copy(src, dst, kind, peer).start()

    def exchange(src, dst, kind, start):
        def one(i, carry):
            copy = state_copy(src, dst, kind, lax.rem(rank + i, size))
            copy.start() if start else copy.wait_send()
            return carry

        lax.fori_loop(1, size, one, 0)

    def arrived(src, dst, kind):
        def one(i, carry):
            peer = lax.rem(rank + i, size)
            pltpu.make_async_remote_copy(
                src_ref=src(rank), dst_ref=dst(peer),
                send_sem=a_send_sem.at[kind, rank], recv_sem=a_recv_sem.at[kind, peer],
                device_id=at_seq(team * size + peer), device_id_type=MESH,
            ).wait_recv()
            return carry

        lax.fori_loop(1, size, one, 0)

    def pair_of(ref):
        return lambda owner: ref.at[pl.ds(owner * share, share)]

    def slot_of(ref):
        return lambda owner: ref.at[owner]

    def team_total(kind):
        return pltpu.make_async_remote_copy(
            src_ref=x_send.at[kind], dst_ref=x_recv.at[kind],
            send_sem=x_send_sem.at[kind], recv_sem=x_recv_sem.at[kind],
            device_id=at_seq((1 - team) * size + rank), device_id_type=MESH,
        )

    def running(first_team, kind, source, low_send, low_own, backwards):
        @pl.when(team == first_team)
        def _():
            x_recv[kind] = jnp.zeros(x_recv.shape[1:], jnp.float32)

        @pl.when(team != first_team)
        def _():
            team_total(kind).wait_recv()

        def one(i, total):
            at = size - 1 - i if backwards else i
            low_send[at] = total.astype(jnp.bfloat16)
            return total + source[at].astype(jnp.float32)

        x_send[kind] = lax.fori_loop(0, size, one, x_recv[kind])
        low_own[pl.ds(rank * share, share)] = low_send[rank]

        @pl.when(team == first_team)
        def _():
            team_total(kind).start()

    g_copy = pltpu.make_async_remote_copy(
        src_ref=g_ref, dst_ref=g_all.at[core], send_sem=g_sem.at[0], recv_sem=g_sem.at[1],
        device_id=(me, other), device_id_type=MESH,
    )
    g_copy.start()
    exchange(pair_of(st_send), slot_of(st_recv), 0, True)

    def piece(block, part, sems, target, own=False):
        span = pl.ds(part * half, half)
        return pltpu.make_async_remote_copy(
            src_ref=w_ref.at[span] if own else w_all.at[block, span],
            dst_ref=w_all.at[block, span],
            send_sem=sems.at[block, part], recv_sem=w_recv_sem.at[block, part],
            device_id=at_seq(target), device_id_type=MESH,
        )

    up_ok = level + 1 < planes
    down_ok = level > 0
    up = jnp.minimum(me + PLANE, blocks - PLANE + spot)
    down = jnp.maximum(me - PLANE, spot)

    for part in range(2):
        piece(me, part, wx_sem, nbr_x, True).start()
        piece(me, part, wy_sem, nbr_y, True).start()

        @pl.when(up_ok)
        def _():
            piece(me, part, wz_sem.at[0], up, True).start()

        @pl.when(down_ok)
        def _():
            piece(me, part, wz_sem.at[1], down, True).start()

    tables = visit_tables(planes)
    order = [pick([tables[z][k] for z in range(planes)], level) for k in range(planes)]

    def passing(k):
        return jnp.where(order[k] < level, up_ok, down_ok)

    def along_z(k, where, finish=False):
        plane = order[k]
        block = plane * PLANE + where
        going_up = plane < level
        for part in range(2):
            for sems, way, go in ((wz_sem.at[0], up, going_up), (wz_sem.at[1], down, jnp.logical_not(going_up))):

                @pl.when(jnp.logical_and(go, passing(k)))
                def _():
                    copy = piece(block, part, sems, way)
                    if finish:
                        copy.wait_send()
                    else:
                        copy.wait_recv()
                        copy.start()

    def end_of_z(k, where, part):
        @pl.when(jnp.logical_not(passing(k)))
        def _():
            piece(order[k] * PLANE + where, part, wx_sem, nbr_x).wait_recv()

    def across(k, finish=False):
        block = order[k] * PLANE + spot
        for part in range(2):
            if not finish:
                end_of_z(k, spot, part)
            for copy in (piece(block, part, wx_sem, nbr_x), piece(block, part, wy_sem, nbr_y)):
                copy.wait_send() if finish else copy.start()

    def relay_step(k, finish=False):
        plane = order[k]
        to_x = piece(plane * PLANE + spot_y, 0, wx_sem, nbr_x)
        to_y = piece(plane * PLANE + spot_x, 1, wy_sem, nbr_y)
        for copy in (to_x, to_y):
            if finish:
                copy.wait_send()
            else:
                copy.wait_recv()
                copy.start()

    def cross_step(k, finish=False):
        block = order[k] * PLANE + spot_d
        for part in range(2):

            @pl.when(level == half_planes - 1)
            def _():
                copy = piece(block, part, wz_sem.at[0], up)
                copy.wait_send() if finish else copy.start()

            @pl.when(level == half_planes)
            def _():
                copy = piece(block, part, wz_sem.at[1], down)
                copy.wait_send() if finish else copy.start()

    def settle(k):
        plane = order[k]
        near = ((spot_y, 1), (spot_x, 0), (spot_d, 0), (spot_d, 1))
        far = ((spot_y, 0), (spot_x, 0), (spot_y, 1), (spot_x, 1))
        for where, part in near if k < half_planes else far:
            piece(plane * PLANE + where, part, wx_sem, nbr_x).wait_recv()
        if k >= half_planes:
            for part in range(2):
                end_of_z(k, spot_d, part)

    causal = lower_mask(length)

    def score_step(h, carry):
        c = head_cols(h)
        kept = jnp.where(causal, contract_cols(q_ref[:, c], k_ref[:, c]), 0.0).astype(jnp.bfloat16)
        weights[h] = kept
        normed[h] = contract_mid(kept, v_ref[:, c])
        return carry

    def norm_step(h, carry):
        c = head_cols(h)
        numerator = normed[h] + contract_mid(q_ref[:, c], prefix[h])
        inv = 1.0 / jnp.sqrt(jnp.mean(numerator * numerator, axis=-1, keepdims=True) + 1e-06)
        value = numerator * inv
        normed[h] = value
        inv_spread[h] = jnp.broadcast_to(inv, (length, HEAD_DIM))
        attended[:, c] = value.astype(jnp.bfloat16)
        return carry

    tile = cols
    n_tiles = rows // tile

    def grad_cols(block):
        return g_all[block // per_core, :, pl.ds(pl.multiple_of(lax.rem(block, per_core) * cols, cols), cols)]

    def direction_step(k):
        base = order[k] * PLANE

        def one(n, carry):
            span = pl.ds(pl.multiple_of(n * tile, tile), tile)
            total = contract_cols(grad_cols(base), w_all[base, span])
            for s in range(1, PLANE):
                total = total + contract_cols(grad_cols(base + s), w_all[base + s, span])
            if k > 0:
                total = total + out_dir[:, span]
            out_dir[:, span] = total
            return carry

        lax.fori_loop(0, n_tiles, one, 0)

    def p_copy(slot):
        return pltpu.make_async_remote_copy(
            src_ref=p_send.at[slot], dst_ref=p_recv.at[slot],
            send_sem=p_send_sem.at[slot], recv_sem=p_recv_sem.at[slot],
            device_id=(me, other), device_id_type=MESH,
        )

    def partial_step(k):
        def one(s, carry):
            block = order[k] * PLANE + s
            term = contract_mid(attended[...], w_all[block]).astype(jnp.bfloat16)
            slot = lax.rem(block, per_core)

            @pl.when(block // per_core == core)
            def _():
                p_own[slot] = term

            @pl.when(block // per_core != core)
            def _():
                p_send[slot] = term
                p_copy(slot).start()

            return carry

        lax.fori_loop(0, PLANE, one, 0)

    q_load.wait()
    lax.fori_loop(0, heads, score_step, 0)
    relay_step(0)
    along_z(1, spot)
    across(1)
    along_z(2, spot)
    arrived(pair_of(st_send), slot_of(st_recv), 0)
    running(0, 0, st_recv, pre_send, prefix, False)
    exchange(slot_of(pre_send), pair_of(prefix), 1, True)
    settle(0)
    cross_step(0)
    along_z(3, spot)
    relay_step(1)
    across(2)
    own_w.wait()
    own_g.wait()
    g_copy.wait()
    direction_step(0)
    along_z(2, spot_d)
    settle(1)
    cross_step(1)
    across(3)
    direction_step(1)
    arrived(slot_of(pre_send), pair_of(prefix), 1)
    lax.fori_loop(0, heads, norm_step, 0)
    partial_step(0)
    along_z(3, spot_d)
    partial_step(1)
    settle(2)
    direction_step(2)
    partial_step(2)
    settle(3)
    direction_step(3)

    def numer_step(h, carry):
        c = head_cols(h)
        toward, unit = out_dir[:, c], normed[h]
        along = jnp.mean(toward * unit, axis=-1, keepdims=True)
        low = ((toward - unit * along) * inv_spread[h]).astype(jnp.bfloat16)
        ng[:, c] = low
        lg_send[h] = contract_rows(q_ref[:, c], low).astype(jnp.bfloat16)

        @pl.when(jnp.logical_and(h > 0, lax.rem(h, share) == 0))
        def _():
            leave(pair_of(lg_send), slot_of(lg_recv), 2, h // share - 1)

        return carry

    lax.fori_loop(0, heads, numer_step, 0)
    leave(pair_of(lg_send), slot_of(lg_recv), 2, size - 1)
    lg_recv[rank] = lg_send[pl.ds(rank * share, share)]
    partial_step(planes - 1)
    arrived(pair_of(lg_send), slot_of(lg_recv), 2)
    running(1, 1, lg_recv, suf_send, suffix, True)
    exchange(slot_of(suf_send), pair_of(suffix), 3, True)

    def pair_step(h, carry):
        c = head_cols(h)
        low = ng[:, c]
        pair = jnp.where(causal, contract_cols(low, v_ref[:, c]), 0.0).astype(jnp.bfloat16)
        dq_ref[:, c] = (contract_mid(pair, k_ref[:, c]) + contract_cols(low, prefix[h])).astype(jnp.bfloat16)
        k_part[h] = contract_rows(pair, q_ref[:, c])
        v_part[h] = contract_rows(weights[h], low)
        return carry

    lax.fori_loop(0, heads, pair_step, 0)

    def mix_step(slot, carry):
        p_copy(slot).wait()
        c = pl.ds(pl.multiple_of(slot * cols, cols), cols)
        mixed_ref[:, c] = (p_own[slot].astype(jnp.float32) + p_recv[slot].astype(jnp.float32)).astype(jnp.bfloat16)
        return carry

    lax.fori_loop(0, per_core, mix_step, 0)
    arrived(slot_of(suf_send), pair_of(suffix), 3)

    def last_step(h, carry):
        c = head_cols(h)
        dk_ref[:, c] = (k_part[h] + contract_cols(v_ref[:, c], suffix[h])).astype(jnp.bfloat16)
        dv_ref[:, c] = (v_part[h] + contract_mid(k_ref[:, c], suffix[h])).astype(jnp.bfloat16)
        return carry

    lax.fori_loop(0, heads, last_step, 0)

    for part in range(2):
        piece(me, part, wx_sem, nbr_x, True).wait_send()
        piece(me, part, wy_sem, nbr_y, True).wait_send()

        @pl.when(up_ok)
        def _():
            piece(me, part, wz_sem.at[0], up, True).wait_send()

        @pl.when(down_ok)
        def _():
            piece(me, part, wz_sem.at[1], down, True).wait_send()

    for k in range(1, planes):
        along_z(k, spot, True)
        across(k, True)
    for k in range(half_planes):
        relay_step(k, True)
        cross_step(k, True)
    for k in range(half_planes, planes):
        along_z(k, spot_d, True)
    exchange(pair_of(st_send), slot_of(st_recv), 0, False)
    exchange(slot_of(pre_send), pair_of(prefix), 1, False)
    exchange(pair_of(lg_send), slot_of(lg_recv), 2, False)
    exchange(slot_of(suf_send), pair_of(suffix), 3, False)
    for kind in range(2):

        @pl.when(team == kind)
        def _():
            team_total(kind).wait_send()


def store_kernel(*refs):
    count = (len(refs) - 1) // 2
    copies = [pltpu.make_async_copy(refs[i], refs[count + i], refs[-1].at[i]) for i in range(count)]
    for copy in copies:
        copy.start()
    for copy in copies:
        copy.wait()


def store(*arrays):
    count = len(arrays)
    return pl.pallas_call(
        store_kernel,
        out_shape=tuple(jax.ShapeDtypeStruct(a.shape, a.dtype) for a in arrays),
        in_specs=[pl.BlockSpec(memory_space=pltpu.VMEM)] * count,
        out_specs=(pl.BlockSpec(memory_space=pltpu.HBM),) * count,
        scratch_shapes=[pltpu.SemaphoreType.DMA((count,))],
        compiler_params=pltpu.CompilerParams(vmem_limit_bytes=8 * 2**20),
    )(*arrays)


def fused(blocks, queries, key_rows, values, out_weight, out_grad):
    length, width = queries.shape
    heads = width // HEAD_DIM
    rows, cols = out_weight.shape
    per_core = blocks // 2
    low, wide = jnp.bfloat16, jnp.float32
    size = blocks // 2
    share = heads // size
    state = pltpu.VMEM((heads, HEAD_DIM, HEAD_DIM), low)
    slots = pltpu.VMEM((size, share, HEAD_DIM, HEAD_DIM), low)
    totals = pltpu.VMEM((2, share, HEAD_DIM, HEAD_DIM), wide)
    by_head = pltpu.VMEM((heads, length, HEAD_DIM), wide)
    flat = pltpu.VMEM((length, width), low)
    parts = pltpu.VMEM((per_core, length, cols), low)
    dma = pltpu.SemaphoreType.DMA
    out = jax.ShapeDtypeStruct((length, width), low)
    vmem, in_hbm = pl.BlockSpec(memory_space=pltpu.VMEM), pl.BlockSpec(memory_space=pltpu.HBM)
    results = pl.pallas_call(
        functools.partial(kernel, blocks),
        out_shape=(out, out, out, out),
        in_specs=[in_hbm] * 5,
        out_specs=(vmem, vmem, vmem, vmem),
        scratch_shapes=[
            flat, flat, flat,
            pltpu.VMEM((blocks, rows, cols), low),
            pltpu.VMEM((2, length, width), low),
            state, slots, slots, state, state, slots, slots, state,
            pltpu.VMEM((length, rows), wide),
            by_head, by_head,
            pltpu.VMEM((heads, length, length), low),
            flat, parts, parts, parts, flat, by_head, by_head,
            totals, totals,
            dma((blocks, 2)), dma((blocks, 2)), dma((blocks, 2)), dma((2, blocks, 2)),
            dma((5,)), dma((2,)), dma((4, blocks)), dma((4, blocks)), dma((per_core,)), dma((per_core,)),
            dma((2,)), dma((2,)),
        ],
        compiler_params=pltpu.CompilerParams(
            collective_id=0, has_side_effects=True, vmem_limit_bytes=49 * 2**20
        ),
    )(queries, key_rows, values, out_weight, out_grad)
    return store(*results)


def solution(mesh):
    blocks, cores = mesh.shape["seq"], mesh.shape["head"]

    def step(queries, key_rows, values, out_weight, out_grad):
        heads = queries.shape[1] // HEAD_DIM
        fits = cores == 2 and blocks == PLANE * PLANE and heads == blocks and out_weight.shape[1] % HEAD_DIM == 0
        fits = fits and out_weight.shape[0] == queries.shape[1] and out_weight.shape[0] % out_weight.shape[1] == 0
        if fits and out_weight.shape[1] * blocks == queries.shape[1] * cores:
            return fused(blocks, queries, key_rows, values, out_weight, out_grad)
        return per_device(queries, key_rows, values, out_weight, out_grad)

    placed = (
        P("seq", "head"),
        P("seq", "head"),
        P("seq", "head"),
        P("head", "seq"),
        P("seq", "head"),
    )
    return jax.shard_map(
        step,
        mesh=mesh,
        in_specs=placed,
        out_specs=(P("seq", "head"), P("seq", "head"), P("seq", "head"), P("seq", "head")),
        check_vma=False,
    )
```
